256 devices in a mesh: ctx: 32 (over x, y, core), mp: 8 (over z).
Axes of the slice: x: 4, y: 4, z: 8, core: 2. Of those that a mesh axis runs over, the one named last changes fastest.
Arguments:
- tokens: bfloat16 [1, 16384, 4096], P(None, 'ctx', 'mp'), may hold values from -40 to 40
- w_branch: bfloat16 [4096, 2048], P(None, 'mp'), may hold values from -0.09375 to 0.09375
- w_input: bfloat16 [4096, 2048], P(None, 'mp'), may hold values from -0.09375 to 0.09375
- conv_kernel: float32 [4, 2048], P(None, 'mp'), may hold values from -3 to 3
- w_rate: bfloat16 [8, 256, 256], P('mp'), may hold values from -0.375 to 0.375
- w_admit: bfloat16 [8, 256, 256], P('mp'), may hold values from -0.375 to 0.375
- lam: float32 [2048], P('mp'), may hold values from 3 to 16
- w_out: bfloat16 [2048, 4096], P('mp'), may hold values from -0.375 to 0.375
- w_query: bfloat16 [4096, 2048], P(None, 'mp'), may hold values from -0.0625 to 0.0625
- w_key: bfloat16 [4096, 256], P(None, 'mp'), may hold values from -4.0625 to 4.0625
- w_value: bfloat16 [4096, 256], P(None, 'mp'), may hold values from -0.09375 to 0.09375
- w_attn_out: bfloat16 [2048, 4096], P('mp'), may hold values from -0.25 to 0.25
Outputs:
- layer_output: bfloat16 [1, 16384, 4096], P(None, 'ctx', 'mp')
The draws below stay inside these ranges and needn't reach their ends.
All inputs are finite; a program needn't handle non-finite values.
Results may differ from the reference program's by a relative error of at most 0.0065.
Values may be sent and summed in bfloat16 or wider, within the bound.
No kernel may reach another device: no remote copies, remote signals or barrier semaphores. Data moves between devices by JAX's collectives and lax.ppermute only.
A program may use at most 128 MiB of HBM per device.

```python
import math
import jax
import jax.numpy as jnp
from jax import lax

D = 4096
LRU = 2048
BW = 256
NB = 8
HEADS = 8
HD = 256
CONV = 4
S_DEV = 512
WINDOW = 2048
B = 1
SEQ = 16384


def draw_tokens(key, part):
    base = jax.random.normal(jax.random.fold_in(key, 1), (B, SEQ, D), jnp.float32)
    base = jnp.clip(base, -4.0, 4.0)
    low = math.log(0.3)
    high = math.log(3.0)
    row_scale = jnp.exp(jax.random.uniform(jax.random.fold_in(key, 2), (B, SEQ, 1), jnp.float32, low, high))
    col_scale = jnp.exp(jax.random.uniform(jax.random.fold_in(key, 3), (1, 1, D), jnp.float32, low, high))
    return (base * row_scale * col_scale).astype(jnp.bfloat16)


def draw_lam(key, part):
    share = 0.5
    pick = jax.random.uniform(jax.random.fold_in(key, 21), (LRU,), jnp.float32)
    quick = 1.0 / jax.random.uniform(jax.random.fold_in(key, 22), (LRU,), jnp.float32, 30.0, 50.0)
    slow = jnp.exp(jax.random.uniform(jax.random.fold_in(key, 23), (LRU,), jnp.float32, math.log(0.2), math.log(2.0))) / SEQ
    rate = jnp.where(pick < share, quick, slow)
    return -jnp.log(jnp.expm1(rate / 4.0))


def query_matrix(key):
    drawn = jnp.clip(jax.random.normal(jax.random.fold_in(key, 31), (D, HEADS * HD), jnp.float32), -4.0, 4.0)
    return drawn / math.sqrt(D)


def draw_w_query(key, part):
    return query_matrix(key).astype(jnp.bfloat16)


def draw_w_key(key, part):
    own = jnp.clip(jax.random.normal(jax.random.fold_in(key, 32), (D, HD), jnp.float32), -4.0, 4.0) / math.sqrt(D)
    return own.astype(jnp.bfloat16)


def block_scale(own_key, dims, cuts, smallest, largest):
    factor_of = 1.0
    for dim, shards_of in cuts:
        heights = jax.random.uniform(jax.random.fold_in(jax.random.fold_in(own_key, 6), dim), (shards_of,), jnp.float32, smallest / len(cuts), largest / len(cuts))
        factor_of = factor_of * jnp.repeat(jnp.exp(heights), dims[dim] // shards_of).reshape((-1,) + (1,) * (len(dims) - 1 - dim))
    return factor_of


def scatter_about(rng, dims, scale, most, split=(), kind=jnp.bfloat16):
    values = scale * jax.random.normal(rng, dims, jnp.float32)
    if split:
        values = values * block_scale(rng, dims, split, -0.22, 0.18)
    return jnp.clip(values, -most, most).astype(kind)


def setup_inputs(seed: int = 0) -> dict:
    arg_keys = jax.random.split(jax.random.key(seed), 13)
    return {
        "tokens": draw_tokens(jax.random.fold_in(arg_keys[12], 71), 0),
        "w_branch": scatter_about(arg_keys[1], (D, LRU), D ** -0.5, 0.09375, ((1, 8),)),
        "w_input": scatter_about(arg_keys[2], (D, LRU), D ** -0.5, 0.09375, ((1, 8),)),
        "conv_kernel": scatter_about(arg_keys[3], (CONV, LRU), CONV ** -0.5, 3.0, ((1, 8),), jnp.float32),
        "w_rate": scatter_about(arg_keys[4], (NB, BW, BW), BW ** -0.5, 0.375, ((0, 8),)),
        "w_admit": scatter_about(arg_keys[5], (NB, BW, BW), BW ** -0.5, 0.375, ((0, 8),)),
        "lam": draw_lam(jax.random.fold_in(arg_keys[12], 71), 0),
        "w_out": scatter_about(arg_keys[7], (LRU, D), (LRU // 8) ** -0.5, 0.375, ((0, 8),)),
        "w_query": draw_w_query(jax.random.fold_in(arg_keys[12], 71), 0),
        "w_key": draw_w_key(jax.random.fold_in(arg_keys[12], 71), 0),
        "w_value": scatter_about(arg_keys[10], (D, HD), D ** -0.5, 0.09375, ((1, 8),)),
        "w_attn_out": scatter_about(arg_keys[11], (HEADS * HD, D), (HEADS * HD // 4) ** -0.5, 0.25, ((0, 8),)),
    }


def normalize(values):
    wide = values.astype(jnp.float32)
    return wide * lax.rsqrt(lax.optimization_barrier(jnp.mean(wide * wide, axis=-1, keepdims=True)) + 1e-06)

def rounded(values):
    return lax.optimization_barrier(values.astype(jnp.bfloat16)).astype(jnp.float32)

def rotate(values, positions):
    width = values.shape[-1]
    turned = width // 2
    half = turned // 2
    freqs = 10000.0 ** (-jnp.arange(half, dtype=jnp.float32) * 2.0 / turned)
    angles = positions.astype(jnp.float32)[:, None] * freqs[None, :]
    cosine = jnp.cos(angles)[:, None, :]
    sine = jnp.sin(angles)[:, None, :]
    first = values[..., :half]
    second = values[..., half:turned]
    return jnp.concatenate([first * cosine - second * sine, second * cosine + first * sine, values[..., turned:]], axis=-1)

def reference(tokens, w_branch, w_input, conv_kernel, w_rate, w_admit, lam, w_out, w_query, w_key, w_value, w_attn_out):
    count = B * SEQ
    normed = normalize(tokens).astype(jnp.bfloat16).reshape(count, D)
    branch = jax.nn.gelu(jnp.dot(normed, w_branch, preferred_element_type=jnp.float32))
    inner = jnp.dot(normed, w_input, preferred_element_type=jnp.float32).reshape(B, SEQ, LRU)
    padded = jnp.pad(inner, ((0, 0), (CONV - 1, 0), (0, 0)))
    convolved = jnp.zeros((B, SEQ, LRU), jnp.float32)
    for tap in range(CONV):
        convolved = convolved + conv_kernel[tap] * padded[:, CONV - 1 - tap:CONV - 1 - tap + SEQ, :]
    grouped = rounded(convolved).reshape(B, SEQ, NB, BW)
    rate_gate = jax.nn.sigmoid(jnp.einsum('bsnc,ncd->bsnd', grouped, w_rate.astype(jnp.float32))).reshape(B, SEQ, LRU)
    admit_gate = jax.nn.sigmoid(jnp.einsum('bsnc,ncd->bsnd', grouped, w_admit.astype(jnp.float32))).reshape(B, SEQ, LRU)
    log_decay = -8.0 * rate_gate * jax.nn.softplus(-lam)
    decay = jnp.exp(log_decay)
    scaled = admit_gate * convolved * jnp.sqrt(-jnp.expm1(2.0 * log_decay))

    def advance(carried, inputs):
        step_decay, step_input = inputs
        fresh = step_decay * carried + step_input
        return (fresh, fresh)
    _, states = lax.scan(advance, jnp.zeros((B, LRU), jnp.float32), (decay.transpose(1, 0, 2), scaled.transpose(1, 0, 2)))
    state = states.transpose(1, 0, 2)
    gated = (state.reshape(count, LRU) * branch).astype(jnp.bfloat16)
    resid = (tokens.reshape(count, D).astype(jnp.float32) + jnp.dot(gated, w_out, preferred_element_type=jnp.float32)).astype(jnp.bfloat16)
    normed_two = normalize(resid).astype(jnp.bfloat16)
    positions = jnp.arange(SEQ, dtype=jnp.int32)
    query = jnp.dot(normed_two, w_query, preferred_element_type=jnp.float32).reshape(B, SEQ, HEADS, HD)
    query = (rotate(query, positions) * HD ** (-0.5)).astype(jnp.bfloat16)
    key_raw = jnp.dot(normed_two, w_key, preferred_element_type=jnp.float32).astype(jnp.bfloat16)
    keys = rotate(key_raw.astype(jnp.float32).reshape(B, SEQ, 1, HD), positions).astype(jnp.bfloat16).reshape(B, SEQ, HD)
    values = jnp.dot(normed_two, w_value, preferred_element_type=jnp.float32).astype(jnp.bfloat16).reshape(B, SEQ, HD)
    key_pad = jnp.pad(keys, ((0, 0), (WINDOW, 0), (0, 0)))
    value_pad = jnp.pad(values, ((0, 0), (WINDOW, 0), (0, 0)))
    span = WINDOW + S_DEV

    def one_block(index):
        start = (index * S_DEV).astype(jnp.int32)
        query_block = lax.dynamic_slice_in_dim(query, start, S_DEV, 1).astype(jnp.float32)
        key_block = lax.dynamic_slice_in_dim(key_pad, start, span, 1).astype(jnp.float32)
        value_block = lax.dynamic_slice_in_dim(value_pad, start, span, 1).astype(jnp.float32)
        scores = jnp.einsum('bshc,bkc->bhsk', query_block, key_block)
        rows = jnp.arange(S_DEV, dtype=jnp.int32)[:, None]
        cols = jnp.arange(span, dtype=jnp.int32)[None, :]
        distance = rows + WINDOW - cols
        valid = (distance >= 0) & (distance < WINDOW) & (cols >= WINDOW - start)
        masked = jnp.where(valid, scores, -1e+30)
        top = lax.optimization_barrier(jnp.max(masked, axis=-1, keepdims=True))
        weights = jnp.where(valid, jnp.exp(masked - top), 0.0)
        probs = rounded(weights / lax.optimization_barrier(jnp.sum(weights, axis=-1, keepdims=True)))
        return jnp.einsum('bhsk,bkc->bshc', probs, value_block).astype(jnp.bfloat16)
    blocks = lax.map(one_block, jnp.arange(SEQ // S_DEV, dtype=jnp.int32))
    attended = blocks.transpose(1, 0, 2, 3, 4).reshape(count, HEADS * HD)
    result = resid.astype(jnp.float32) + jnp.dot(attended, w_attn_out, preferred_element_type=jnp.float32)
    return result.astype(jnp.bfloat16).reshape(B, SEQ, D)
```

```python
import jax
import jax.numpy as jnp
from jax import lax
from jax.experimental import pallas as pl
from jax.experimental.pallas import tpu as pltpu
from jax.sharding import PartitionSpec as P

HD = 256
WINDOW = 2048
EPSILON = 1e-06
BF = jnp.bfloat16
F32 = jnp.float32
VMEM_BYTES = 56 * 1024 * 1024


def around(x, axis, by):
    count = lax.axis_size(axis)
    return lax.ppermute(x, axis, [(i, (i + by) % count) for i in range(count)])


def from_behind(x, axis, by):
    count = lax.axis_size(axis)
    pairs = [(i, i + by) for i in range(count) if 0 <= i + by < count]
    return lax.ppermute(x, axis, pairs)


def ring_chunks(x, axis):
    count = lax.axis_size(axis)
    half = count // 2
    ahead, back = x, x
    found = [(0, x)]
    for step in range(1, half):
        ahead = around(ahead, axis, 1)
        back = around(back, axis, -1)
        found.append((step, ahead))
        found.append((count - step, back))
    cut = x.shape[0] // 2
    top = around(ahead[:cut], axis, 1)
    low = around(back[cut:], axis, -1)
    found.append((half, jnp.concatenate([top, low], axis=0)))
    return found


def place(w, axis, behind):
    count = lax.axis_size(axis)
    index = lax.rem(lax.axis_index(axis) + (count - behind), count)
    return lax.dynamic_index_in_dim(w, index, 0, keepdims=False)


def dot32(a, b):
    return jnp.dot(a, b, preferred_element_type=F32)


def small_expm1(y):
    near = y * (
        1.0
        + y * (1 / 2)
        * (1.0 + y * (1 / 3) * (1.0 + y * (1 / 4) * (1.0 + y * (1 / 5) * (1.0 + y * (1 / 6)
        * (1.0 + y * (1 / 7) * (1.0 + y * (1 / 8) * (1.0 + y * (1 / 9) * (1.0 + y * (1 / 10)))))))))
    )
    return jnp.where(y > -1.0, near, jnp.exp(y) - 1.0)


def scan_body(both, squares, halo, taps, w_rate, w_admit, rate_scale, lsb, cub, ends, ext, dec, sca, lanes_in):
    rows = both.shape[0]
    wide = lanes_in
    r = lax.rsqrt(squares[...] * (1.0 / 4096.0) + EPSILON)
    ext[0:8, :] = halo[...]
    ext[8 : 8 + rows, :] = both[:, wide : 2 * wide] * r
    conv = taps[0:1, :] * ext[8 : 8 + rows, :]
    for tap in range(1, 4):
        conv = conv + taps[tap : tap + 1, :] * ext[8 - tap : 8 - tap + rows, :]
    low = conv.astype(BF)
    rate = jax.nn.sigmoid(dot32(low, w_rate[...]))
    log_decay = rate * rate_scale[...]
    decay = jnp.exp(log_decay)
    admit = jax.nn.sigmoid(dot32(low, w_admit[...]))
    scaled = admit * conv * jnp.sqrt(-small_expm1(2.0 * log_decay))
    seg = rows // 8
    parts = range(wide // 128)
    for n in parts:
        dec[n][...] = decay[:, n * 128 : (n + 1) * 128]
        sca[n][...] = scaled[:, n * 128 : (n + 1) * 128]
    c = [dec[n][pl.ds(0, 8, stride=seg), :] for n in parts]
    h = [sca[n][pl.ds(0, 8, stride=seg), :] for n in parts]
    for t in range(1, seg):
        for n in parts:
            d = dec[n][pl.ds(t, 8, stride=seg), :]
            h[n] = d * h[n] + sca[n][pl.ds(t, 8, stride=seg), :]
            c[n] = c[n] * d
            dec[n][pl.ds(t, 8, stride=seg), :] = c[n]
            sca[n][pl.ds(t, 8, stride=seg), :] = h[n]
    c, h = jnp.concatenate(c, axis=1), jnp.concatenate(h, axis=1)
    before_h = jnp.zeros((1, wide), F32)
    before_c = jnp.ones((1, wide), F32)
    for g in range(8):
        at = slice(g * seg, (g + 1) * seg)
        branch = jax.nn.gelu(both[at, 0:wide] * r[at])
        cum = jnp.concatenate([dec[n][at, :] for n in parts], axis=1)
        state = jnp.concatenate([sca[n][at, :] for n in parts], axis=1)
        lsb[at, :] = (state + cum * before_h) * branch
        cub[at, :] = cum * before_c * branch
        before_h = h[g : g + 1, :] + c[g : g + 1, :] * before_h
        before_c = c[g : g + 1, :] * before_c
    ends[0:1, :] = before_c
    ends[1:2, :] = before_h


def local_scan(both, squares, halo, taps, w_rate, w_admit, rate_scale):
    rows, wide = both.shape[0], both.shape[1] // 2

    def body(*refs):
        scan_body(*refs, wide)

    return pl.pallas_call(
        body,
        out_shape=(
            jax.ShapeDtypeStruct((rows, wide), F32),
            jax.ShapeDtypeStruct((rows, wide), F32),
            jax.ShapeDtypeStruct((2, wide), F32),
        ),
        scratch_shapes=[
            pltpu.VMEM((rows + 8, wide), F32),
            [pltpu.VMEM((rows, 128), F32)] * (wide // 128),
            [pltpu.VMEM((rows, 128), F32)] * (wide // 128),
        ],
        compiler_params=pltpu.CompilerParams(vmem_limit_bytes=VMEM_BYTES),
        name="local_scan",
    )(both, squares, halo, taps, w_rate, w_admit, rate_scale)


def apply_carry(lsb, cub, pieces, mine):
    def body(at, lsb, cub, pieces, out):
        carry = jnp.zeros((1, lsb.shape[1]), F32)
        for k in range(pieces.shape[0]):
            fresh = pieces[k, 1:2, :] + pieces[k, 0:1, :] * carry
            carry = jnp.where(k < at[0], fresh, carry)
        out[...] = (lsb[...] + cub[...] * carry).astype(BF)

    vm = pl.BlockSpec(memory_space=pltpu.VMEM)
    return pl.pallas_call(
        body,
        in_specs=[pl.BlockSpec(memory_space=pltpu.SMEM), vm, vm, vm],
        out_specs=vm,
        out_shape=jax.ShapeDtypeStruct(lsb.shape, BF),
        compiler_params=pltpu.CompilerParams(vmem_limit_bytes=VMEM_BYTES),
        name="apply_carry",
    )(mine, lsb, cub, pieces)


def attention(q_raw, own, other, bias, cos_k, sin_k, cos_q, sin_q):
    rows = q_raw.shape[0]
    span = bias.shape[1]
    slots = ((own, 2), (other, 1), (own, 1), (other, 0), (own, 0))
    quarter = HD // 4
    each = HD // own.shape[0]

    def body(q_raw, own, other, bias, cos_k, sin_k, cos_q, sin_q, out, kt, vt, qs):
        refs = ((own, 2), (other, 1), (own, 1), (other, 0), (own, 0))
        for b, (ref, slot) in enumerate(refs):
            at = slice(slot * rows, (slot + 1) * rows)
            to = slice(b * rows, (b + 1) * rows)
            total = jnp.zeros((1, rows), F32)
            for z in range(own.shape[0]):
                total = total + ref[z, 2 * each : 2 * each + 1, at].astype(F32)
                total = total + ref[z, 2 * each + 1 : 2 * each + 2, at].astype(F32)
            r = lax.rsqrt(total * (1.0 / 4096.0) + EPSILON)
            raw = jnp.concatenate([ref[z, 0:each, at] for z in range(HD // 2 // each)], axis=0).astype(F32) * r
            first, second = raw[0:quarter], raw[quarter : 2 * quarter]
            c, s = cos_k[:, to], sin_k[:, to]
            kt[0:quarter, to] = (first * c - second * s).astype(BF)
            kt[quarter : 2 * quarter, to] = (second * c + first * s).astype(BF)
            for z in range(own.shape[0]):
                if z >= HD // 2 // each:
                    kt[z * each : (z + 1) * each, to] = (ref[z, 0:each, at].astype(F32) * r).astype(BF)
                vt[z * each : (z + 1) * each, to] = (ref[z, each : 2 * each, at].astype(F32) * r).astype(BF)
        turned = []
        for b in range(rows // 128):
            square = jnp.broadcast_to(r[:, b * 128 : (b + 1) * 128], (128, 128))
            turned.append(square.T)
        r_rows = jnp.concatenate(turned, axis=0) * (HD**-0.5)
        head = q_raw[:, 0:128] * r_rows
        spun = pltpu.roll(head, quarter, 1)
        qs[:, 0:128] = (head * cos_q[...] + spun * sin_q[...]).astype(BF)
        qs[:, 128:256] = (q_raw[:, 128:256] * r_rows).astype(BF)
        row = lax.broadcasted_iota(jnp.int32, (128, 128), 0)
        col = lax.broadcasted_iota(jnp.int32, (128, 128), 1)
        for b in range(rows // 128):
            start = b * 128
            width = WINDOW + 128
            s = dot32(qs[start : start + 128, :], kt[:, start : start + width]) + bias[:, start : start + width]
            lead = jnp.where(col > row, s[:, 0:128], -1e30)
            tail = jnp.where(col <= row, s[:, WINDOW:width], -1e30)
            s = jnp.concatenate([lead, s[:, 128:WINDOW], tail], axis=1)
            top = jnp.max(s, axis=1, keepdims=True)
            p = jnp.exp(s - top)
            total = jnp.sum(p, axis=1, keepdims=True)
            o = lax.dot_general(
                p.astype(BF), vt[:, start : start + width], (((1,), (1,)), ((), ())), preferred_element_type=F32
            )
            out[start : start + 128, :] = (o / total).astype(BF)

    del slots
    return pl.pallas_call(
        body,
        out_shape=jax.ShapeDtypeStruct((rows, HD), BF),
        scratch_shapes=[
            pltpu.VMEM((HD, span), BF),
            pltpu.VMEM((HD, span), BF),
            pltpu.VMEM((rows, HD), BF),
        ],
        compiler_params=pltpu.CompilerParams(vmem_limit_bytes=VMEM_BYTES),
        name="attention",
    )(q_raw, own, other, bias, cos_k, sin_k, cos_q, sin_q)


def on_device(
    tokens, w_branch, w_input, conv_kernel, w_rate, w_admit, lam, w_out, w_query, w_key, w_value, w_attn_out
):
    batch, rows, cols = tokens.shape
    width = w_branch.shape[0]
    n_mp, n_ctx = lax.axis_size("mp"), lax.axis_size("ctx")
    z, j = lax.axis_index("mp"), lax.axis_index("ctx")
    lru = w_branch.shape[1]
    x = tokens.reshape(rows, cols)

    part = w_out.shape[0] // n_ctx
    mine = jnp.concatenate(
        [lax.dynamic_slice_in_dim(w_out, j * part, part, 0), lax.dynamic_slice_in_dim(w_attn_out, j * part, part, 0)],
        axis=0,
    )
    lines = lax.all_gather(mine, "mp", axis=0)
    out_lines = lines[:, :part].reshape(n_mp * part, width)
    attn_lines = lines[:, part:].reshape(n_mp * part, width)
    w_qkv = jnp.concatenate([w_query, w_key, w_value], axis=1)
    n_qkv = w_qkv.shape[1]
    joined = dot32(out_lines, w_qkv).astype(BF)
    own_cols = lax.dynamic_slice_in_dim(out_lines, z * cols, cols, 1)
    payload = jnp.concatenate([joined, own_cols], axis=1)

    def along_ctx(a):
        whole = lax.all_gather(a, "ctx", axis=0)
        whole = whole.reshape(n_ctx, n_mp, part, a.shape[1]).transpose(1, 0, 2, 3)
        return whole.reshape(n_mp, n_ctx * part, a.shape[1])

    w_second = along_ctx(payload)
    w_last = along_ctx(lax.dynamic_slice_in_dim(attn_lines, z * cols, cols, 1))

    w_first = jnp.concatenate([w_branch, w_input], axis=1).reshape(n_mp, cols, 2 * lru)
    w_qkv = w_qkv.reshape(n_mp, cols, n_qkv)
    both = qkv = squares = 0.0
    for behind, chunk in ring_chunks(x, "mp"):
        wide = chunk.astype(F32)
        squares = squares + jnp.sum(wide * wide, axis=1, keepdims=True)
        both = both + dot32(chunk, place(w_first, "mp", behind))
        qkv = qkv + dot32(chunk, place(w_qkv, "mp", behind))
    tail = both[rows - 8 :, lru:] * lax.rsqrt(squares[rows - 8 :] / width + EPSILON)
    halo = from_behind(tail, "ctx", 1)
    rate_scale = (-8.0 * jax.nn.softplus(-lam)).reshape(1, lru)
    lsb, cub, ends = local_scan(both, squares, halo, conv_kernel, w_rate[0], w_admit[0], rate_scale)
    copies = jnp.broadcast_to(ends, (n_ctx, *ends.shape))
    pieces = lax.all_to_all(copies, "ctx", split_axis=0, concat_axis=0, tiled=True)
    gated = apply_carry(lsb, cub, pieces, j.reshape(1))

    second = jnp.concatenate([qkv, x.astype(F32)], axis=1)
    for behind, chunk in ring_chunks(gated, "mp"):
        second = second + dot32(chunk, place(w_second, "mp", behind))
    q_raw = second[:, :HD]
    kv = second[:, HD:n_qkv]
    resid = second[:, n_qkv:].astype(BF)
    wide = resid.astype(F32)
    partial = jnp.sum(wide * wide, axis=1)
    high = partial.astype(BF)
    low = (partial - high.astype(F32)).astype(BF)
    block = jnp.concatenate(
        [kv.astype(BF).T, high[None], low[None], jnp.zeros((14, rows), BF)], axis=0
    )

    line = jnp.concatenate([block, from_behind(block, "ctx", 2), from_behind(block, "ctx", 4)], axis=1)
    own = jnp.zeros((n_mp, *line.shape), BF)
    for behind, chunk in ring_chunks(line, "mp"):
        index = lax.rem(z + (n_mp - behind), n_mp)
        own = lax.dynamic_update_index_in_dim(own, chunk, index, 0)
    core = lax.rem(j, 2)
    sent = lax.dynamic_slice_in_dim(own, core * rows, 2 * rows, 2)
    other = lax.ppermute(sent, "ctx", [(i, i ^ 1) for i in range(n_ctx)])

    base = j * rows
    span = WINDOW + rows
    half = HD // 4
    freqs = 10000.0 ** (-jnp.arange(half, dtype=F32) * 2.0 / (HD // 2))
    where = (base - WINDOW + jnp.arange(span, dtype=jnp.int32)).astype(F32)
    angles = freqs[:, None] * where[None, :]
    cos_k, sin_k = jnp.cos(angles), jnp.sin(angles)
    cos_own, sin_own = cos_k[:, WINDOW:].T, sin_k[:, WINDOW:].T
    cos_q = jnp.concatenate([cos_own, cos_own], axis=1)
    sin_q = jnp.concatenate([-sin_own, sin_own], axis=1)
    bias = jnp.where(jnp.arange(span, dtype=jnp.int32) >= WINDOW - base, 0.0, -1e30).astype(F32)[None]
    attended = attention(q_raw, own, other, bias, cos_k, sin_k, cos_q, sin_q)

    last = wide
    for behind, chunk in ring_chunks(attended, "mp"):
        last = last + dot32(chunk, place(w_last, "mp", behind))
    return last.astype(BF).reshape(batch, rows, cols)


def solution(mesh):
    in_specs = (
        P(None, "ctx", "mp"),
        P(None, "mp"),
        P(None, "mp"),
        P(None, "mp"),
        P("mp", None, None),
        P("mp", None, None),
        P("mp"),
        P("mp", None),
        P(None, "mp"),
        P(None, "mp"),
        P(None, "mp"),
        P("mp", None),
    )
    return jax.shard_map(
        on_device, mesh=mesh, in_specs=in_specs, out_specs=P(None, "ctx", "mp"), check_vma=False
    )
```

```python
import jax
import jax.numpy as jnp
from jax import lax
from jax.experimental import pallas as pl
from jax.experimental.pallas import tpu as pltpu
from jax.sharding import PartitionSpec as P

HD = 256
WINDOW = 2048
EPSILON = 1e-06
BF = jnp.bfloat16
F32 = jnp.float32
VMEM_BYTES = 16 * 1024 * 1024


def around(x, axis, by):
    count = lax.axis_size(axis)
    return lax.ppermute(x, axis, [(i, (i + by) % count) for i in range(count)])


def from_behind(x, axis, by):
    count = lax.axis_size(axis)
    pairs = [(i, i + by) for i in range(count) if 0 <= i + by < count]
    return lax.ppermute(x, axis, pairs)


def dot32(a, b):
    return jnp.dot(a, b, preferred_element_type=F32)


def ring_pieces(x, axis, cut, works=None):
    count = lax.axis_size(axis)
    half = count // 2
    works = works or {}
    made = {}
    parts = [x]

    moving = [(p, p) for p in parts]
    found = {0: parts}
    for step in range(1, half):
        arrived = [(around(a, axis, 1), around(b, axis, -1)) for a, b in moving]
        if step in works:
            made[step] = works[step](dict(found), made)
            arrived, made[step] = lax.optimization_barrier((arrived, made[step]))
        moving = arrived
        found[step] = [a for a, _ in moving]
        found[count - step] = [b for _, b in moving]
    (a, b), size = moving[0], x.shape[cut] // 2
    a, b = lax.slice_in_dim(a, 0, size, axis=cut), lax.slice_in_dim(b, size, 2 * size, axis=cut)
    last = lax.optimization_barrier([around(a, axis, 1), around(b, axis, -1)])
    if half in works:
        made[half] = works[half](dict(found), made)
        last, made[half] = lax.optimization_barrier((last, made[half]))
    found[half] = last
    return found, made


def nearest(pieces, count, distance):
    return {k: v for k, v in pieces.items() if min(k, count - k) <= distance}


def others(pieces, some):
    return {k: v for k, v in pieces.items() if k not in some}


VM = pl.BlockSpec(memory_space=pltpu.VMEM)
SM = pl.BlockSpec(memory_space=pltpu.SMEM)
BIG = pltpu.CompilerParams(vmem_limit_bytes=VMEM_BYTES)
STEP = 256


def chunk_call(name, z, pieces, extra, outs, finish, count, weights, rows):
    behinds = list(pieces)
    flat = [p for k in behinds for p in pieces[k]]

    several = [k for k in behinds if len(pieces[k]) > 1]
    deep = pieces[behinds[0]][0].shape[1]

    def body(z, *refs):
        refs = list(refs)
        whole = refs.pop()
        took = {}
        for k in behinds:
            took[k] = [refs.pop(0) for _ in pieces[k]]
        for n, k in enumerate(several):
            at = 0
            for ref in took[k]:
                used = min(ref.shape[0], rows - at)
                whole[n, at : at + used, :] = ref[0:used, :]
                at += used
            took[k] = [whole.at[n]]
        w = [refs.pop(0) for _ in weights]
        more = [refs.pop(0) for _ in extra]

        def step(i, _):
            here = pl.ds(pl.multiple_of(i * STEP, STEP), STEP)
            chunks = [took[k][0][here, :] for k in behinds]
            dots = [0.0] * len(w)
            for k, chunk in zip(behinds, chunks):
                at = pl.multiple_of(lax.rem(z[0] + (count - k), count) * deep, deep)
                for n, ref in enumerate(w):
                    dots[n] = dots[n] + dot32(chunk, ref[pl.ds(at, deep), :])
            finish(i, here, dots, more, refs, chunks)
            return 0

        lax.fori_loop(0, rows // STEP, step, 0)

    return pl.pallas_call(
        body,
        in_specs=[SM] + [VM] * (len(flat) + len(weights) + len(extra)),
        out_specs=tuple(VM for _ in outs),
        out_shape=tuple(outs),
        scratch_shapes=[pltpu.VMEM((max(len(several), 1), rows, deep), BF)],
        compiler_params=BIG,
        name=name,
    )(z, *flat, *weights, *extra)


def first_dots(z, pieces, before, count, w_branch, w_input, rows):
    n = w_branch.shape[1]
    outs = [jax.ShapeDtypeStruct((rows, n), F32)] * 2 + [jax.ShapeDtypeStruct((rows, 1), F32)]
    final = before is not None
    if final:
        outs = outs + [jax.ShapeDtypeStruct((8, n), F32)]

    def finish(i, here, dots, more, out, chunks):
        squares = 0.0
        for chunk in chunks:
            for c in range(0, chunk.shape[1], 128):
                wide = chunk[:, c : c + 128].astype(F32)
                squares = squares + wide * wide
        squares = jnp.sum(squares, axis=1, keepdims=True)
        if final:
            dots = [d + m[here, :] for d, m in zip(dots, more)]
            squares = squares + more[2][here, :]
        out[0][here, :] = dots[0]
        out[1][here, :] = dots[1]
        out[2][here, :] = squares
        if final:
            r = lax.rsqrt(squares[STEP - 8 :] * (1.0 / 4096.0) + EPSILON)
            out[3][...] = dots[1][STEP - 8 :] * r

    return chunk_call("first_dots", z, pieces, list(before or ()), outs, finish, count, [w_branch, w_input], rows)


def one_dot(name, z, pieces, before, count, w, rows):

    def finish(i, here, dots, more, out, chunks):
        out[0][here, :] = dots[0] + more[0][here, :] if more else dots[0]

    outs = [jax.ShapeDtypeStruct((rows, w.shape[1]), F32)]
    return chunk_call(name, z, pieces, [] if before is None else [before], outs, finish, count, [w], rows)[0]


def middle(z, pieces, before, qkv, x, count, w, each):
    rows, cols = x.shape
    outs = [
        jax.ShapeDtypeStruct((rows, HD), F32),
        jax.ShapeDtypeStruct((80, rows), BF),
        jax.ShapeDtypeStruct((rows, cols), BF),
    ]

    def finish(i, here, dots, more, out, chunks):
        d = dots[0] + more[0][here, :]
        out[0][here, :] = d[:, 0:HD] + more[1][here, 0:HD]
        resid = (d[:, HD + 128 :] + more[2][here, :].astype(F32)).astype(BF)
        out[2][here, :] = resid
        wide = resid.astype(F32)
        squares = jnp.sum(wide * wide, axis=1, keepdims=True)
        kv = d[:, HD : HD + 128] + more[1][here, HD : HD + 128]
        lane = lax.broadcasted_iota(jnp.int32, kv.shape, 1)
        turned = jnp.where(lane == 2 * each, squares, kv).T
        out[1][0 : 2 * each, here] = turned[0 : 2 * each].astype(BF)
        line = turned[2 * each : 2 * each + 16]
        main = line.astype(BF).astype(F32)
        row = lax.broadcasted_iota(jnp.int32, line.shape, 0)
        low_part = jnp.broadcast_to((line - main)[0:1], line.shape)
        both = jnp.where(row == 0, main, jnp.where(row == 1, low_part, 0.0))
        out[1][2 * each : 2 * each + 16, here] = both.astype(BF)

    return chunk_call("middle", z, pieces, [before, qkv, x], outs, finish, count, [w], rows)


def last_dot(z, pieces, before, resid, count, w):
    rows = resid.shape[0]

    def finish(i, here, dots, more, out, chunks):
        out[0][here, :] = (dots[0] + more[0][here, :] + more[1][here, :].astype(F32)).astype(BF)

    outs = [jax.ShapeDtypeStruct(resid.shape, BF)]
    return chunk_call("last_dot", z, pieces, [before, resid], outs, finish, count, [w], rows)[0]


def line_products(z, pieces, count, w, part):
    behinds = list(pieces)
    cols = pieces[behinds[0]][0].shape[1]
    n = w.shape[1]

    def body(z, *refs):
        *took, w, out, out_last, lines = refs
        for k, ref in zip(behinds, took):
            at = pl.multiple_of(lax.rem(z[0] + (count - k), count) * part, part)
            for c in range(2 * count):
                first = pieces[k][1] + c * part
                lines[c, pl.ds(at, part), :] = ref[first : first + part, :].astype(F32)
        total = 0.0
        for c in range(count):
            total = total + dot32(lines[c].astype(BF), w[c * cols : (c + 1) * cols, :])
        out[:, 0:n] = total.astype(BF)
        out[:, n : n + cols] = lines[z[0]].astype(BF)
        out_last[...] = lines[z[0] + count].astype(BF)

    return pl.pallas_call(
        body,
        in_specs=[SM] + [VM] * (len(behinds) + 1),
        out_specs=(VM, VM),
        out_shape=(
            jax.ShapeDtypeStruct((part * count, n + cols), BF),
            jax.ShapeDtypeStruct((part * count, cols), BF),
        ),
        scratch_shapes=[pltpu.VMEM((2 * count, part * count, cols), F32)],
        compiler_params=BIG,
        name="line_products",
    )(z, *[pieces[k][0] for k in behinds], w)


def window(z, core, near, far, cos, sin, count, each):
    rows = cos.shape[1] // 3
    behinds = list(near)
    flat = [p for k in behinds for p in near[k] + far[k]]
    quarter = HD // 4

    def body(z, core, *refs):
        refs = list(refs)
        raw_all, kv, sent, r_out = refs[-1], refs[-4], refs[-3], refs[-2]
        cos, sin = refs[-6], refs[-5]
        for k in behinds:
            index = lax.rem(z[0] + (count - k), count)
            at = 0
            for _ in near[k] + far[k]:
                ref = refs.pop(0)
                raw_all[index, :, at : at + ref.shape[1]] = ref[...]
                at += ref.shape[1]
        for slot in range(3):
            at = slice(slot * rows, (slot + 1) * rows)
            total = jnp.zeros((1, rows), F32)
            for k in range(count):
                total = total + raw_all[k, 2 * each : 2 * each + 1, at].astype(F32)
                total = total + raw_all[k, 2 * each + 1 : 2 * each + 2, at].astype(F32)
            r = lax.rsqrt(total * (1.0 / 4096.0) + EPSILON)
            if slot == 0:
                r_out[...] = jnp.broadcast_to(r, r_out.shape)
            n = HD // 2 // each
            head = jnp.concatenate([raw_all[k, 0:each, at] for k in range(n)], axis=0).astype(F32) * r
            first, second = head[0:quarter], head[quarter : 2 * quarter]
            c, s = cos[:, at], sin[:, at]
            done = [(0, first * c - second * s), (quarter, second * c + first * s)]
            for k in range(count):
                if k >= n:
                    done.append((k * each, raw_all[k, 0:each, at].astype(F32) * r))
                done.append((HD + k * each, raw_all[k, each : 2 * each, at].astype(F32) * r))
            for start, value in done:
                value = value.astype(BF)
                kv[start : start + value.shape[0], at] = value
                to = slice(start, start + value.shape[0])

                if slot == 0:
                    @pl.when(core[0] == 0)
                    def _():
                        sent[to, 0:rows] = value
                elif slot == 1:
                    @pl.when(core[0] == 0)
                    def _():
                        sent[to, rows : 2 * rows] = value

                    @pl.when(core[0] == 1)
                    def _():
                        sent[to, 0:rows] = value
                else:
                    @pl.when(core[0] == 1)
                    def _():
                        sent[to, rows : 2 * rows] = value

    return pl.pallas_call(
        body,
        in_specs=[SM, SM] + [VM] * (len(flat) + 2),
        out_specs=(VM, VM, VM),
        out_shape=(
            jax.ShapeDtypeStruct((2 * HD, 3 * rows), BF),
            jax.ShapeDtypeStruct((2 * HD, 2 * rows), BF),
            jax.ShapeDtypeStruct((8, rows), F32),
        ),
        scratch_shapes=[pltpu.VMEM((count, 80, 3 * rows), BF)],
        compiler_params=BIG,
        name="window",
    )(z, core, *flat, cos, sin)


def make_query(q_raw, r, cos_q, sin_q):
    rows = q_raw.shape[0]

    def body(q_raw, r, cos_q, sin_q, out):
        turned = []
        for b in range(rows // 128):
            turned.append(jnp.broadcast_to(r[0:1, b * 128 : (b + 1) * 128], (128, 128)).T)
        scale = jnp.concatenate(turned, axis=0) * (HD**-0.5)
        head = q_raw[:, 0:128] * scale
        spun = pltpu.roll(head, HD // 4, 1)
        out[:, 0:128] = (head * cos_q[...] + spun * sin_q[...]).astype(BF)
        out[:, 128:256] = (q_raw[:, 128:256] * scale).astype(BF)

    return pl.pallas_call(
        body, out_shape=jax.ShapeDtypeStruct(q_raw.shape, BF), compiler_params=BIG, name="make_query"
    )(q_raw, r, cos_q, sin_q)


def attention(query, own, other, bias):
    rows = query.shape[0]
    width = WINDOW + 128

    def body(query, own, other, bias, out, kv):
        for n, (ref, slot) in enumerate(((own, 2), (other, 1), (own, 1), (other, 0), (own, 0))):
            kv[:, n * rows : (n + 1) * rows] = ref[:, slot * rows : (slot + 1) * rows]
        row = lax.broadcasted_iota(jnp.int32, (128, 128), 0)
        col = lax.broadcasted_iota(jnp.int32, (128, 128), 1)

        def block(b, _):
            start = pl.multiple_of(b * 128, 128)
            seen = pl.ds(start, width)
            s = dot32(query[pl.ds(start, 128), :], kv[0:HD, seen]) + bias[:, seen]
            lead = jnp.where(col > row, s[:, 0:128], -1e30)
            tail = jnp.where(col <= row, s[:, WINDOW:width], -1e30)
            s = jnp.concatenate([lead, s[:, 128:WINDOW], tail], axis=1)
            top = jnp.max(s, axis=1, keepdims=True)
            p = jnp.exp(s - top)
            total = jnp.sum(p, axis=1, keepdims=True)
            o = lax.dot_general(
                p.astype(BF), kv[HD : 2 * HD, seen], (((1,), (1,)), ((), ())), preferred_element_type=F32
            )
            out[pl.ds(start, 128), :] = (o / total).astype(BF)
            return 0

        lax.fori_loop(0, rows // 128, block, 0)

    return pl.pallas_call(
        body,
        out_shape=jax.ShapeDtypeStruct((rows, HD), BF),
        scratch_shapes=[pltpu.VMEM((2 * HD, WINDOW + rows), BF)],
        compiler_params=BIG,
        name="attention",
    )(query, own, other, bias)


def small_expm1(y):
    near = y * (
        1.0
        + y * (1 / 2)
        * (1.0 + y * (1 / 3) * (1.0 + y * (1 / 4) * (1.0 + y * (1 / 5) * (1.0 + y * (1 / 6)
        * (1.0 + y * (1 / 7) * (1.0 + y * (1 / 8) * (1.0 + y * (1 / 9) * (1.0 + y * (1 / 10)))))))))
    )
    return jnp.where(y > -1.0, near, jnp.exp(y) - 1.0)


def scan_body(to_branch, inner, squares, halo, taps, w_rate, w_admit, rate_scale, lsb, cub, ends, ext, prior, dec, sca, lanes_in):
    rows = inner.shape[0]
    wide = lanes_in
    ext[0:8, :] = halo[...]
    seg = rows // 8
    parts = range(wide // 128)

    def scaled_in(i, _):
        here = pl.ds(pl.multiple_of(i * 128, 128), 128)
        r = lax.rsqrt(squares[here, :] * (1.0 / 4096.0) + EPSILON)
        ext[pl.ds(pl.multiple_of(i * 128 + 8, 8), 128), :] = inner[here, :] * r
        return 0

    lax.fori_loop(0, rows // 128, scaled_in, 0)

    def gates(i, _):
        here = pl.ds(pl.multiple_of(i * 128, 128), 128)
        around_here = ext[pl.ds(pl.multiple_of(i * 128, 128), 136), :]
        conv = taps[0:1, :] * around_here[8:136]
        for tap in range(1, 4):
            conv = conv + taps[tap : tap + 1, :] * around_here[8 - tap : 136 - tap]
        low = conv.astype(BF)
        rate = jax.nn.sigmoid(dot32(low, w_rate[...]))
        log_decay = rate * rate_scale[...]
        decay = jnp.exp(log_decay)
        admit = jax.nn.sigmoid(dot32(low, w_admit[...]))
        scaled = admit * conv * jnp.sqrt(-small_expm1(2.0 * log_decay))
        for n in parts:
            dec[n][here, :] = decay[:, n * 128 : (n + 1) * 128]
            sca[n][here, :] = scaled[:, n * 128 : (n + 1) * 128]
        return 0

    lax.fori_loop(0, rows // 128, gates, 0)
    c = [dec[n][pl.ds(0, 8, stride=seg), :] for n in parts]
    h = [sca[n][pl.ds(0, 8, stride=seg), :] for n in parts]
    for t in range(1, seg):
        for n in parts:
            d = dec[n][pl.ds(t, 8, stride=seg), :]
            h[n] = d * h[n] + sca[n][pl.ds(t, 8, stride=seg), :]
            c[n] = c[n] * d
            dec[n][pl.ds(t, 8, stride=seg), :] = c[n]
            sca[n][pl.ds(t, 8, stride=seg), :] = h[n]
    c, h = jnp.concatenate(c, axis=1), jnp.concatenate(h, axis=1)
    before_h = jnp.zeros((1, wide), F32)
    before_c = jnp.ones((1, wide), F32)
    befores = []
    for g in range(8):
        befores.append((before_h, before_c))
        before_h = h[g : g + 1, :] + c[g : g + 1, :] * before_h
        before_c = c[g : g + 1, :] * before_c
    prior[0:8, :] = jnp.concatenate([p[0] for p in befores], axis=0)
    prior[8:16, :] = jnp.concatenate([p[1] for p in befores], axis=0)

    def joined(g, _):
        here = pl.ds(pl.multiple_of(g * seg, seg), seg)
        r = lax.rsqrt(squares[here, :] * (1.0 / 4096.0) + EPSILON)
        branch = jax.nn.gelu(to_branch[here, :] * r)
        cum = jnp.concatenate([dec[n][here, :] for n in parts], axis=1)
        state = jnp.concatenate([sca[n][here, :] for n in parts], axis=1)
        lsb[here, :] = (state + cum * prior[pl.ds(g, 1), :]) * branch
        cub[here, :] = cum * prior[pl.ds(g + 8, 1), :] * branch
        return 0

    lax.fori_loop(0, 8, joined, 0)
    for k in range(ends.shape[0]):
        ends[k, 0:1, :] = before_c
        ends[k, 1:2, :] = before_h


def local_scan(to_branch, inner, squares, halo, taps, w_rate, w_admit, rate_scale, copies):
    rows, wide = inner.shape

    def body(*refs):
        scan_body(*refs, wide)

    return pl.pallas_call(
        body,
        out_shape=(
            jax.ShapeDtypeStruct((rows, wide), F32),
            jax.ShapeDtypeStruct((rows, wide), F32),
            jax.ShapeDtypeStruct((copies, 2, wide), F32),
        ),
        scratch_shapes=[
            pltpu.VMEM((rows + 8, wide), F32),
            pltpu.VMEM((16, wide), F32),
            [pltpu.VMEM((rows, 128), F32)] * (wide // 128),
            [pltpu.VMEM((rows, 128), F32)] * (wide // 128),
        ],
        compiler_params=pltpu.CompilerParams(vmem_limit_bytes=VMEM_BYTES),
        name="local_scan",
    )(to_branch, inner, squares, halo, taps, w_rate, w_admit, rate_scale)


def apply_carry(lsb, cub, pieces, mine):
    def body(at, lsb, cub, pieces, out):
        carry = jnp.zeros((1, lsb.shape[1]), F32)
        for k in range(pieces.shape[0]):
            fresh = pieces[k, 1:2, :] + pieces[k, 0:1, :] * carry
            carry = jnp.where(k < at[0], fresh, carry)
        out[...] = (lsb[...] + cub[...] * carry).astype(BF)

    vm = pl.BlockSpec(memory_space=pltpu.VMEM)
    return pl.pallas_call(
        body,
        in_specs=[pl.BlockSpec(memory_space=pltpu.SMEM), vm, vm, vm],
        out_specs=vm,
        out_shape=jax.ShapeDtypeStruct(lsb.shape, BF),
        compiler_params=pltpu.CompilerParams(vmem_limit_bytes=VMEM_BYTES),
        name="apply_carry",
    )(mine, lsb, cub, pieces)


def on_device(
    tokens, w_branch, w_input, conv_kernel, w_rate, w_admit, lam, w_out, w_query, w_key, w_value, w_attn_out
):
    batch, rows, cols = tokens.shape
    width = w_branch.shape[0]
    n_mp, n_ctx = lax.axis_size("mp"), lax.axis_size("ctx")
    z, j = lax.axis_index("mp"), lax.axis_index("ctx")
    lru = w_branch.shape[1]
    x = tokens.reshape(rows, cols)

    zs, cores = z.reshape(1), lax.rem(j, 2).reshape(1)
    half = n_mp // 2
    each = w_key.shape[1]
    part = w_out.shape[0] // n_ctx

    def lines_of(w):
        return lax.dynamic_slice_in_dim(w, j * part, part, 0)

    def along_ctx(a):
        return lax.all_gather(a, "ctx", axis=0)

    def in_order(a):
        whole = a.reshape(n_ctx, n_mp, part, a.shape[-1]).transpose(1, 0, 2, 3)
        return whole.reshape(n_mp * n_ctx * part, a.shape[-1])

    lines = jnp.stack([lines_of(w_out), lines_of(w_attn_out)]).reshape(2, part, n_mp, cols)
    lines = lines.transpose(0, 2, 1, 3).reshape(2 * n_mp * part, cols)

    def joined_weights(found, made):
        return jnp.concatenate([w_query, w_key, w_value, jnp.zeros((width, 128 - 2 * each), BF)], axis=1)

    def tables(found, made):
        base, _ = lax.optimization_barrier((j * rows, found[1][0]))
        span = WINDOW + rows
        freqs = 10000.0 ** (-jnp.arange(HD // 4, dtype=F32) * 2.0 / (HD // 2))
        slots = jnp.concatenate([jnp.arange(rows, dtype=jnp.int32) - back * rows for back in (0, 2, 4)])
        angles = freqs[:, None] * (base + slots).astype(F32)[None, :]
        cos_k, sin_k = jnp.cos(angles), jnp.sin(angles)
        cos_own, sin_own = cos_k[:, :rows].T, sin_k[:, :rows].T
        cos_q = jnp.concatenate([cos_own, cos_own], axis=1)
        sin_q = jnp.concatenate([-sin_own, sin_own], axis=1)
        bias = jnp.where(jnp.arange(span, dtype=jnp.int32) >= WINDOW - base, 0.0, -1e30).astype(F32)[None]
        rate_scale = (-8.0 * jax.nn.softplus(-lam)).reshape(1, lru)
        return cos_k, sin_k, cos_q, sin_q, bias, rate_scale

    def first_part(found, made):
        return first_dots(zs, found, None, n_mp, w_branch, w_input, rows)

    of_x, made = ring_pieces(jnp.concatenate([x, lines], axis=0), "mp", 0, {1: joined_weights, 2: tables, 3: first_part})
    w_qkv = made[1]
    cos_k, sin_k, cos_q, sin_q, bias, rate_scale = made[2]
    near_x = nearest(of_x, n_mp, half - 2)
    to_branch, inner, squares, tail = first_dots(zs, others(of_x, near_x), made[3], n_mp, w_branch, w_input, rows)
    halo = from_behind(tail, "ctx", 1)

    with_lines = {k: (v[-1], rows - (0 if len(v) == 1 else v[0].shape[0])) for k, v in of_x.items()}
    products, last_lines = line_products(zs, with_lines, n_mp, w_qkv, part)
    w_second = along_ctx(products)
    w_last = along_ctx(last_lines)

    lsb, cub, ends = local_scan(
        to_branch, inner, squares, halo, conv_kernel, w_rate[0], w_admit[0], rate_scale, n_ctx
    )
    carried = lax.all_to_all(ends, "ctx", split_axis=0, concat_axis=0, tiled=True)
    gated = apply_carry(lsb, cub, carried, j.reshape(1))

    def after(value, found):
        flat, tree = jax.tree.flatten(value)
        *flat, _ = lax.optimization_barrier((*flat, found[0][0]))
        return jax.tree.unflatten(tree, flat)

    def some_of_x(found, made):
        return one_dot("first_qkv", zs, after(near_x, found), None, n_mp, w_qkv, rows)

    def rest_of_x(found, made):
        return one_dot("first_qkv", zs, others(of_x, near_x), made[1], n_mp, w_qkv, rows)

    def second_weights(found, made):
        return in_order(after(w_second, {0: [found[1][0]]}))

    def some_second(found, made):
        return one_dot("second", zs, nearest(found, n_mp, half - 2), None, n_mp, made[3], rows)

    pieces, made = ring_pieces(
        gated, "mp", 0, {1: some_of_x, 2: rest_of_x, 3: second_weights, 4: some_second}
    )
    late = others(pieces, nearest(pieces, n_mp, half - 2))
    q_raw, block, resid = middle(zs, late, made[4], made[2], x, n_mp, made[3], each)

    def last_weights(found, made):
        return in_order(after(w_last, {0: [found[2][0]]}))

    line = jnp.concatenate([block, from_behind(block, "ctx", 2), from_behind(block, "ctx", 4)], axis=1)
    near, made = ring_pieces(line, "mp", 1, {3: last_weights})
    w_last = made[3]
    own, sent, r = window(zs, cores, near, {k: [] for k in near}, cos_k, sin_k, n_mp, each)
    other = lax.ppermute(sent, "ctx", [(i, i ^ 1) for i in range(n_ctx)])
    query = make_query(q_raw, r, cos_q, sin_q)
    attended = attention(query, own, other, bias)

    def some_last(found, made):
        return one_dot("third", zs, nearest(found, n_mp, half - 2), None, n_mp, w_last, rows)

    pieces, made = ring_pieces(attended, "mp", 0, {3: some_last})
    late = others(pieces, nearest(pieces, n_mp, half - 2))
    last = last_dot(zs, late, made[3], resid, n_mp, w_last)
    return last.reshape(batch, rows, cols)


def solution(mesh):
    in_specs = (
        P(None, "ctx", "mp"),
        P(None, "mp"),
        P(None, "mp"),
        P(None, "mp"),
        P("mp", None, None),
        P("mp", None, None),
        P("mp"),
        P("mp", None),
        P(None, "mp"),
        P(None, "mp"),
        P(None, "mp"),
        P("mp", None),
    )
    return jax.shard_map(
        on_device, mesh=mesh, in_specs=in_specs, out_specs=P(None, "ctx", "mp"), check_vma=False
    )
```

```python
import jax
import jax.numpy as jnp
from jax import lax
from jax.experimental import pallas as pl
from jax.experimental.pallas import tpu as pltpu
from jax.sharding import PartitionSpec as P

HD = 256
WINDOW = 2048
EPSILON = 1e-06
BF = jnp.bfloat16
F32 = jnp.float32
VMEM_BYTES = 16 * 1024 * 1024


def around(x, axis, by):
    count = lax.axis_size(axis)
    return lax.ppermute(x, axis, [(i, (i + by) % count) for i in range(count)])


def from_behind(x, axis, by):
    count = lax.axis_size(axis)
    pairs = [(i, i + by) for i in range(count) if 0 <= i + by < count]
    return lax.ppermute(x, axis, pairs)


def dot32(a, b):
    return jnp.dot(a, b, preferred_element_type=F32)


def ring_pieces(x, axis, cut, works=None):
    count = lax.axis_size(axis)
    half = count // 2
    works = works or {}
    made = {}
    parts = [x]

    moving = [(p, p) for p in parts]
    found = {0: parts}
    for step in range(1, half):
        arrived = [(around(a, axis, 1), around(b, axis, -1)) for a, b in moving]
        if step in works:
            made[step] = works[step](dict(found), made)
            arrived, made[step] = lax.optimization_barrier((arrived, made[step]))
        moving = arrived
        found[step] = [a for a, _ in moving]
        found[count - step] = [b for _, b in moving]
    (a, b), size = moving[0], x.shape[cut] // 2
    a, b = lax.slice_in_dim(a, 0, size, axis=cut), lax.slice_in_dim(b, size, 2 * size, axis=cut)
    last = lax.optimization_barrier([around(a, axis, 1), around(b, axis, -1)])
    if half in works:
        made[half] = works[half](dict(found), made)
        last, made[half] = lax.optimization_barrier((last, made[half]))
    found[half] = last
    return found, made


def nearest(pieces, count, distance):
    return {k: v for k, v in pieces.items() if min(k, count - k) <= distance}


def others(pieces, some):
    return {k: v for k, v in pieces.items() if k not in some}


VM = pl.BlockSpec(memory_space=pltpu.VMEM)
SM = pl.BlockSpec(memory_space=pltpu.SMEM)
BIG = pltpu.CompilerParams(vmem_limit_bytes=VMEM_BYTES)
STEP = 256


def chunk_call(name, z, pieces, extra, outs, finish, count, weights, rows):
    behinds = list(pieces)
    flat = [p for k in behinds for p in pieces[k]]

    several = [k for k in behinds if len(pieces[k]) > 1]
    deep = pieces[behinds[0]][0].shape[1]

    def body(z, *refs):
        refs = list(refs)
        whole = refs.pop()
        took = {}
        for k in behinds:
            took[k] = [refs.pop(0) for _ in pieces[k]]
        for n, k in enumerate(several):
            at = 0
            for ref in took[k]:
                used = min(ref.shape[0], rows - at)
                whole[n, at : at + used, :] = ref[0:used, :]
                at += used
            took[k] = [whole.at[n]]
        w = [refs.pop(0) for _ in weights]
        more = [refs.pop(0) for _ in extra]

        def step(i, _):
            here = pl.ds(pl.multiple_of(i * STEP, STEP), STEP)
            chunks = [took[k][0][here, :] for k in behinds]
            dots = [0.0] * len(w)
            for k, chunk in zip(behinds, chunks):
                at = pl.multiple_of(lax.rem(z[0] + (count - k), count) * deep, deep)
                for n, ref in enumerate(w):
                    dots[n] = dots[n] + dot32(chunk, ref[pl.ds(at, deep), :])
            finish(i, here, dots, more, refs, chunks)
            return 0

        lax.fori_loop(0, rows // STEP, step, 0)

    return pl.pallas_call(
        body,
        in_specs=[SM] + [VM] * (len(flat) + len(weights) + len(extra)),
        out_specs=tuple(VM for _ in outs),
        out_shape=tuple(outs),
        scratch_shapes=[pltpu.VMEM((max(len(several), 1), rows, deep), BF)],
        compiler_params=BIG,
        name=name,
    )(z, *flat, *weights, *extra)


def first_dots(z, pieces, before, count, w_branch, w_input, rows):
    n = w_branch.shape[1]
    outs = [jax.ShapeDtypeStruct((rows, n), F32)] * 2 + [jax.ShapeDtypeStruct((rows, 1), F32)]
    final = before is not None
    if final:
        outs = outs + [jax.ShapeDtypeStruct((8, n), F32)]

    def finish(i, here, dots, more, out, chunks):
        squares = 0.0
        for chunk in chunks:
            for c in range(0, chunk.shape[1], 128):
                wide = chunk[:, c : c + 128].astype(F32)
                squares = squares + wide * wide
        squares = jnp.sum(squares, axis=1, keepdims=True)
        if final:
            dots = [d + m[here, :] for d, m in zip(dots, more)]
            squares = squares + more[2][here, :]
        out[0][here, :] = dots[0]
        out[1][here, :] = dots[1]
        out[2][here, :] = squares
        if final:
            r = lax.rsqrt(squares[STEP - 8 :] * (1.0 / 4096.0) + EPSILON)
            out[3][...] = dots[1][STEP - 8 :] * r

    return chunk_call("first_dots", z, pieces, list(before or ()), outs, finish, count, [w_branch, w_input], rows)


def one_dot(name, z, pieces, before, count, w, rows):

    def finish(i, here, dots, more, out, chunks):
        out[0][here, :] = dots[0] + more[0][here, :] if more else dots[0]

    outs = [jax.ShapeDtypeStruct((rows, w.shape[1]), F32)]
    return chunk_call(name, z, pieces, [] if before is None else [before], outs, finish, count, [w], rows)[0]


def middle(z, pieces, before, qkv, x, count, w, each):
    rows, cols = x.shape
    outs = [
        jax.ShapeDtypeStruct((rows, HD), F32),
        jax.ShapeDtypeStruct((80, rows), BF),
        jax.ShapeDtypeStruct((rows, cols), BF),
    ]

    def finish(i, here, dots, more, out, chunks):
        d = dots[0] + more[0][here, :]
        out[0][here, :] = d[:, 0:HD] + more[1][here, 0:HD]
        resid = (d[:, HD + 128 :] + more[2][here, :].astype(F32)).astype(BF)
        out[2][here, :] = resid
        wide = resid.astype(F32)
        squares = jnp.sum(wide * wide, axis=1, keepdims=True)
        kv = d[:, HD : HD + 128] + more[1][here, HD : HD + 128]
        lane = lax.broadcasted_iota(jnp.int32, kv.shape, 1)
        turned = jnp.where(lane == 2 * each, squares, kv).T
        out[1][0 : 2 * each, here] = turned[0 : 2 * each].astype(BF)
        line = turned[2 * each : 2 * each + 16]
        main = line.astype(BF).astype(F32)
        row = lax.broadcasted_iota(jnp.int32, line.shape, 0)
        low_part = jnp.broadcast_to((line - main)[0:1], line.shape)
        both = jnp.where(row == 0, main, jnp.where(row == 1, low_part, 0.0))
        out[1][2 * each : 2 * each + 16, here] = both.astype(BF)

    return chunk_call("middle", z, pieces, [before, qkv, x], outs, finish, count, [w], rows)


def last_dot(z, pieces, before, resid, count, w):
    rows = resid.shape[0]

    def finish(i, here, dots, more, out, chunks):
        out[0][here, :] = (dots[0] + more[0][here, :] + more[1][here, :].astype(F32)).astype(BF)

    outs = [jax.ShapeDtypeStruct(resid.shape, BF)]
    return chunk_call("last_dot", z, pieces, [before, resid], outs, finish, count, [w], rows)[0]


def line_products(z, pieces, count, w, part):
    behinds = list(pieces)
    cols = pieces[behinds[0]][0].shape[1]
    n = w.shape[1]

    def body(z, *refs):
        *took, w, out, out_last, lines = refs
        for k, ref in zip(behinds, took):
            at = pl.multiple_of(lax.rem(z[0] + (count - k), count) * part, part)
            for c in range(2 * count):
                first = pieces[k][1] + c * part
                lines[c, pl.ds(at, part), :] = ref[first : first + part, :].astype(F32)
        total = 0.0
        for c in range(count):
            total = total + dot32(lines[c].astype(BF), w[c * cols : (c + 1) * cols, :])
        out[:, 0:n] = total.astype(BF)
        out[:, n : n + cols] = lines[z[0]].astype(BF)
        out_last[...] = lines[z[0] + count].astype(BF)

    return pl.pallas_call(
        body,
        in_specs=[SM] + [VM] * (len(behinds) + 1),
        out_specs=(VM, VM),
        out_shape=(
            jax.ShapeDtypeStruct((part * count, n + cols), BF),
            jax.ShapeDtypeStruct((part * count, cols), BF),
        ),
        scratch_shapes=[pltpu.VMEM((2 * count, part * count, cols), F32)],
        compiler_params=BIG,
        name="line_products",
    )(z, *[pieces[k][0] for k in behinds], w)


def window(z, core, near, far, cos, sin, count, each):
    rows = cos.shape[1] // 3
    behinds = list(near)
    flat = [p for k in behinds for p in near[k] + far[k]]
    quarter = HD // 4

    def body(z, core, *refs):
        refs = list(refs)
        raw_all, kv, sent, r_out = refs[-1], refs[-4], refs[-3], refs[-2]
        cos, sin = refs[-6], refs[-5]
        for k in behinds:
            index = lax.rem(z[0] + (count - k), count)
            at = 0
            for _ in near[k] + far[k]:
                ref = refs.pop(0)
                raw_all[index, :, at : at + ref.shape[1]] = ref[...]
                at += ref.shape[1]
        for slot in range(3):
            at = slice(slot * rows, (slot + 1) * rows)
            total = jnp.zeros((1, rows), F32)
            for k in range(count):
                total = total + raw_all[k, 2 * each : 2 * each + 1, at].astype(F32)
                total = total + raw_all[k, 2 * each + 1 : 2 * each + 2, at].astype(F32)
            r = lax.rsqrt(total * (1.0 / 4096.0) + EPSILON)
            if slot == 0:
                r_out[...] = jnp.broadcast_to(r, r_out.shape)
            n = HD // 2 // each
            head = jnp.concatenate([raw_all[k, 0:each, at] for k in range(n)], axis=0).astype(F32) * r
            first, second = head[0:quarter], head[quarter : 2 * quarter]
            c, s = cos[:, at], sin[:, at]
            done = [(0, first * c - second * s), (quarter, second * c + first * s)]
            for k in range(count):
                if k >= n:
                    done.append((k * each, raw_all[k, 0:each, at].astype(F32) * r))
                done.append((HD + k * each, raw_all[k, each : 2 * each, at].astype(F32) * r))
            for start, value in done:
                value = value.astype(BF)
                kv[start : start + value.shape[0], at] = value
                to = slice(start, start + value.shape[0])

                if slot == 0:
                    @pl.when(core[0] == 0)
                    def _():
                        sent[to, 0:rows] = value
                elif slot == 1:
                    @pl.when(core[0] == 0)
                    def _():
                        sent[to, rows : 2 * rows] = value

                    @pl.when(core[0] == 1)
                    def _():
                        sent[to, 0:rows] = value
                else:
                    @pl.when(core[0] == 1)
                    def _():
                        sent[to, rows : 2 * rows] = value

    return pl.pallas_call(
        body,
        in_specs=[SM, SM] + [VM] * (len(flat) + 2),
        out_specs=(VM, VM, VM),
        out_shape=(
            jax.ShapeDtypeStruct((2 * HD, 3 * rows), BF),
            jax.ShapeDtypeStruct((2 * HD, 2 * rows), BF),
            jax.ShapeDtypeStruct((8, rows), F32),
        ),
        scratch_shapes=[pltpu.VMEM((count, 80, 3 * rows), BF)],
        compiler_params=BIG,
        name="window",
    )(z, core, *flat, cos, sin)


def make_query(q_raw, r, cos, sin):
    rows = q_raw.shape[0]

    def body(q_raw, r, cos, sin, out):
        for b in range(rows // 128):
            at = slice(b * 128, (b + 1) * 128)
            scale = jnp.broadcast_to(r[0:1, at], (128, 128)).T * (HD**-0.5)
            c, s = cos[:, at], sin[:, at]
            turn_same = jnp.concatenate([c, c], axis=0).T
            turn_other = jnp.concatenate([-s, s], axis=0).T
            head = q_raw[at, 0:128] * scale
            spun = pltpu.roll(head, HD // 4, 1)
            out[at, 0:128] = (head * turn_same + spun * turn_other).astype(BF)
            out[at, 128:256] = (q_raw[at, 128:256] * scale).astype(BF)

    return pl.pallas_call(
        body, out_shape=jax.ShapeDtypeStruct(q_raw.shape, BF), compiler_params=BIG, name="make_query"
    )(q_raw, r, cos, sin)


def attention(query, own, other, bias):
    rows = query.shape[0]
    width = WINDOW + 128

    def body(query, own, other, bias, out, kv):
        for n, (ref, slot) in enumerate(((own, 2), (other, 1), (own, 1), (other, 0), (own, 0))):
            kv[:, n * rows : (n + 1) * rows] = ref[:, slot * rows : (slot + 1) * rows]
        row = lax.broadcasted_iota(jnp.int32, (128, 128), 0)
        col = lax.broadcasted_iota(jnp.int32, (128, 128), 1)

        def block(b, _):
            start = pl.multiple_of(b * 128, 128)
            seen = pl.ds(start, width)
            s = dot32(query[pl.ds(start, 128), :], kv[0:HD, seen]) + bias[:, seen]
            lead = jnp.where(col > row, s[:, 0:128], -1e30)
            tail = jnp.where(col <= row, s[:, WINDOW:width], -1e30)
            s = jnp.concatenate([lead, s[:, 128:WINDOW], tail], axis=1)
            top = jnp.max(s, axis=1, keepdims=True)
            p = jnp.exp(s - top)
            total = jnp.sum(p, axis=1, keepdims=True)
            o = lax.dot_general(
                p.astype(BF), kv[HD : 2 * HD, seen], (((1,), (1,)), ((), ())), preferred_element_type=F32
            )
            out[pl.ds(start, 128), :] = (o / total).astype(BF)
            return 0

        lax.fori_loop(0, rows // 128, block, 0)

    return pl.pallas_call(
        body,
        out_shape=jax.ShapeDtypeStruct((rows, HD), BF),
        scratch_shapes=[pltpu.VMEM((2 * HD, WINDOW + rows), BF)],
        compiler_params=BIG,
        name="attention",
    )(query, own, other, bias)


def small_expm1(y):
    near = y * (
        1.0
        + y * (1 / 2)
        * (1.0 + y * (1 / 3) * (1.0 + y * (1 / 4) * (1.0 + y * (1 / 5) * (1.0 + y * (1 / 6)
        * (1.0 + y * (1 / 7) * (1.0 + y * (1 / 8) * (1.0 + y * (1 / 9) * (1.0 + y * (1 / 10)))))))))
    )
    return jnp.where(y > -1.0, near, jnp.exp(y) - 1.0)


def scan_body(to_branch, inner, squares, halo, taps, w_rate, w_admit, rate_scale, lsb, cub, ends, ext, prior, dec, sca, lanes_in):
    rows = inner.shape[0]
    wide = lanes_in
    ext[0:8, :] = halo[...]
    seg = rows // 8
    parts = range(wide // 128)

    def scaled_in(i, _):
        here = pl.ds(pl.multiple_of(i * 128, 128), 128)
        r = lax.rsqrt(squares[here, :] * (1.0 / 4096.0) + EPSILON)
        ext[pl.ds(pl.multiple_of(i * 128 + 8, 8), 128), :] = inner[here, :] * r
        return 0

    lax.fori_loop(0, rows // 128, scaled_in, 0)

    def gates(i, _):
        here = pl.ds(pl.multiple_of(i * 128, 128), 128)
        around_here = ext[pl.ds(pl.multiple_of(i * 128, 128), 136), :]
        conv = taps[0:1, :] * around_here[8:136]
        for tap in range(1, 4):
            conv = conv + taps[tap : tap + 1, :] * around_here[8 - tap : 136 - tap]
        low = conv.astype(BF)
        rate = jax.nn.sigmoid(dot32(low, w_rate[...]))
        log_decay = rate * rate_scale[...]
        decay = jnp.exp(log_decay)
        admit = jax.nn.sigmoid(dot32(low, w_admit[...]))
        scaled = admit * conv * jnp.sqrt(-small_expm1(2.0 * log_decay))
        for n in parts:
            dec[n][here, :] = decay[:, n * 128 : (n + 1) * 128]
            sca[n][here, :] = scaled[:, n * 128 : (n + 1) * 128]
        return 0

    lax.fori_loop(0, rows // 128, gates, 0)
    c = [dec[n][pl.ds(0, 8, stride=seg), :] for n in parts]
    h = [sca[n][pl.ds(0, 8, stride=seg), :] for n in parts]
    for t in range(1, seg):
        for n in parts:
            d = dec[n][pl.ds(t, 8, stride=seg), :]
            h[n] = d * h[n] + sca[n][pl.ds(t, 8, stride=seg), :]
            c[n] = c[n] * d
            dec[n][pl.ds(t, 8, stride=seg), :] = c[n]
            sca[n][pl.ds(t, 8, stride=seg), :] = h[n]
    c, h = jnp.concatenate(c, axis=1), jnp.concatenate(h, axis=1)
    before_h = jnp.zeros((1, wide), F32)
    before_c = jnp.ones((1, wide), F32)
    befores = []
    for g in range(8):
        befores.append((before_h, before_c))
        before_h = h[g : g + 1, :] + c[g : g + 1, :] * before_h
        before_c = c[g : g + 1, :] * before_c
    prior[0:8, :] = jnp.concatenate([p[0] for p in befores], axis=0)
    prior[8:16, :] = jnp.concatenate([p[1] for p in befores], axis=0)

    def joined(g, _):
        here = pl.ds(pl.multiple_of(g * seg, seg), seg)
        r = lax.rsqrt(squares[here, :] * (1.0 / 4096.0) + EPSILON)
        branch = jax.nn.gelu(to_branch[here, :] * r)
        cum = jnp.concatenate([dec[n][here, :] for n in parts], axis=1)
        state = jnp.concatenate([sca[n][here, :] for n in parts], axis=1)
        lsb[here, :] = (state + cum * prior[pl.ds(g, 1), :]) * branch
        cub[here, :] = cum * prior[pl.ds(g + 8, 1), :] * branch
        return 0

    lax.fori_loop(0, 8, joined, 0)
    for k in range(ends.shape[0]):
        ends[k, 0:1, :] = before_c
        ends[k, 1:2, :] = before_h


def local_scan(to_branch, inner, squares, halo, taps, w_rate, w_admit, rate_scale, copies):
    rows, wide = inner.shape

    def body(*refs):
        scan_body(*refs, wide)

    return pl.pallas_call(
        body,
        out_shape=(
            jax.ShapeDtypeStruct((rows, wide), F32),
            jax.ShapeDtypeStruct((rows, wide), F32),
            jax.ShapeDtypeStruct((copies, 2, wide), F32),
        ),
        scratch_shapes=[
            pltpu.VMEM((rows + 8, wide), F32),
            pltpu.VMEM((16, wide), F32),
            [pltpu.VMEM((rows, 128), F32)] * (wide // 128),
            [pltpu.VMEM((rows, 128), F32)] * (wide // 128),
        ],
        compiler_params=pltpu.CompilerParams(vmem_limit_bytes=VMEM_BYTES),
        name="local_scan",
    )(to_branch, inner, squares, halo, taps, w_rate, w_admit, rate_scale)


def apply_carry(lsb, cub, pieces, mine):
    def body(at, lsb, cub, pieces, out):
        carry = jnp.zeros((1, lsb.shape[1]), F32)
        for k in range(pieces.shape[0]):
            fresh = pieces[k, 1:2, :] + pieces[k, 0:1, :] * carry
            carry = jnp.where(k < at[0], fresh, carry)
        out[...] = (lsb[...] + cub[...] * carry).astype(BF)

    vm = pl.BlockSpec(memory_space=pltpu.VMEM)
    return pl.pallas_call(
        body,
        in_specs=[pl.BlockSpec(memory_space=pltpu.SMEM), vm, vm, vm],
        out_specs=vm,
        out_shape=jax.ShapeDtypeStruct(lsb.shape, BF),
        compiler_params=pltpu.CompilerParams(vmem_limit_bytes=VMEM_BYTES),
        name="apply_carry",
    )(mine, lsb, cub, pieces)


def on_device(
    tokens, w_branch, w_input, conv_kernel, w_rate, w_admit, lam, w_out, w_query, w_key, w_value, w_attn_out
):
    batch, rows, cols = tokens.shape
    width = w_branch.shape[0]
    n_mp, n_ctx = lax.axis_size("mp"), lax.axis_size("ctx")
    z, j = lax.axis_index("mp"), lax.axis_index("ctx")
    z, j, core, base, first_seen, tokens = lax.optimization_barrier(
        (z, j, lax.rem(j, 2), j * rows, WINDOW - j * rows, tokens)
    )
    lru = w_branch.shape[1]
    x = tokens.reshape(rows, cols)

    zs, cores = z.reshape(1), core.reshape(1)
    half = n_mp // 2
    each = w_key.shape[1]
    part = w_out.shape[0] // n_ctx

    def lines_of(w):
        return lax.dynamic_slice_in_dim(w, j * part, part, 0)

    def along_ctx(a):
        return lax.all_gather(a, "ctx", axis=0)

    def in_order(a):
        whole = a.reshape(n_ctx, n_mp, part, a.shape[-1]).transpose(1, 0, 2, 3)
        return whole.reshape(n_mp * n_ctx * part, a.shape[-1])

    lines = jnp.stack([lines_of(w_out), lines_of(w_attn_out)]).reshape(2, part, n_mp, cols)
    lines = lines.transpose(0, 2, 1, 3).reshape(2 * n_mp * part, cols)

    def joined_weights(found, made):
        return jnp.concatenate([w_query, w_key, w_value, jnp.zeros((width, 128 - 2 * each), BF)], axis=1)

    def tables(found, made):
        here, _ = lax.optimization_barrier((base, found[1][0]))
        span = WINDOW + rows
        freqs = 10000.0 ** (-jnp.arange(HD // 4, dtype=F32) * 2.0 / (HD // 2))
        slots = jnp.concatenate([jnp.arange(rows, dtype=jnp.int32) - back * rows for back in (0, 2, 4)])
        angles = freqs[:, None] * (here + slots).astype(F32)[None, :]
        cos_k, sin_k = jnp.cos(angles), jnp.sin(angles)
        bias = jnp.where(jnp.arange(span, dtype=jnp.int32) >= first_seen, 0.0, -1e30).astype(F32)[None]
        rate_scale = (-8.0 * jax.nn.softplus(-lam)).reshape(1, lru)
        return cos_k, sin_k, bias, rate_scale

    def first_part(found, made):
        return first_dots(zs, found, None, n_mp, w_branch, w_input, rows)

    of_x, made = ring_pieces(jnp.concatenate([x, lines], axis=0), "mp", 0, {1: joined_weights, 2: tables, 3: first_part})
    w_qkv = made[1]
    cos_k, sin_k, bias, rate_scale = made[2]
    near_x = nearest(of_x, n_mp, half - 2)
    to_branch, inner, squares, tail = first_dots(zs, others(of_x, near_x), made[3], n_mp, w_branch, w_input, rows)

    with_lines = {k: (v[-1], rows - (0 if len(v) == 1 else v[0].shape[0])) for k, v in of_x.items()}
    zs_late, tail = lax.optimization_barrier((zs, tail))
    products, last_lines = line_products(zs_late, with_lines, n_mp, w_qkv, part)
    w_second = along_ctx(products)
    halo = from_behind(tail, "ctx", 1)

    lsb, cub, ends = local_scan(
        to_branch, inner, squares, halo, conv_kernel, w_rate[0], w_admit[0], rate_scale, n_ctx
    )
    last_lines, ends = lax.optimization_barrier((last_lines, ends))
    w_last = along_ctx(last_lines)
    carried = lax.all_to_all(ends, "ctx", split_axis=0, concat_axis=0, tiled=True)
    gated = apply_carry(lsb, cub, carried, j.reshape(1))

    def after(value, found):
        flat, tree = jax.tree.flatten(value)
        *flat, _ = lax.optimization_barrier((*flat, found[0][0]))
        return jax.tree.unflatten(tree, flat)

    def some_of_x(found, made):
        return one_dot("first_qkv", zs, after(near_x, found), None, n_mp, w_qkv, rows)

    def rest_of_x(found, made):
        return one_dot("first_qkv", zs, others(of_x, near_x), made[1], n_mp, w_qkv, rows)

    def second_weights(found, made):
        return in_order(after(w_second, {0: [found[1][0]]}))

    def some_second(found, made):
        return one_dot("second", zs, nearest(found, n_mp, half - 2), None, n_mp, made[3], rows)

    pieces, made = ring_pieces(
        gated, "mp", 0, {1: some_of_x, 2: rest_of_x, 3: second_weights, 4: some_second}
    )
    late = others(pieces, nearest(pieces, n_mp, half - 2))
    q_raw, block, resid = middle(zs, late, made[4], made[2], x, n_mp, made[3], each)

    def last_weights(found, made):
        return in_order(after(w_last, {0: [found[2][0]]}))

    line = jnp.concatenate([block, from_behind(block, "ctx", 2), from_behind(block, "ctx", 4)], axis=1)
    near, made = ring_pieces(line, "mp", 1, {3: last_weights})
    w_last = made[3]
    own, sent, r = window(zs, cores, near, {k: [] for k in near}, cos_k, sin_k, n_mp, each)
    other = lax.ppermute(sent, "ctx", [(i, i ^ 1) for i in range(n_ctx)])
    query = make_query(q_raw, r, cos_k, sin_k)
    attended = attention(query, own, other, bias)

    def some_last(found, made):
        return one_dot("third", zs, nearest(found, n_mp, half - 2), None, n_mp, w_last, rows)

    pieces, made = ring_pieces(attended, "mp", 0, {3: some_last})
    late = others(pieces, nearest(pieces, n_mp, half - 2))
    last = last_dot(zs, late, made[3], resid, n_mp, w_last)
    return last.reshape(batch, rows, cols)


def solution(mesh):
    in_specs = (
        P(None, "ctx", "mp"),
        P(None, "mp"),
        P(None, "mp"),
        P(None, "mp"),
        P("mp", None, None),
        P("mp", None, None),
        P("mp"),
        P("mp", None),
        P(None, "mp"),
        P(None, "mp"),
        P(None, "mp"),
        P("mp", None),
    )
    return jax.shard_map(
        on_device, mesh=mesh, in_specs=in_specs, out_specs=P(None, "ctx", "mp"), check_vma=False
    )
```

```python
import jax
import jax.numpy as jnp
from jax import lax
from jax.experimental import pallas as pl
from jax.experimental.pallas import tpu as pltpu
from jax.sharding import PartitionSpec as P

HD = 256
WINDOW = 2048
EPSILON = 1e-06
BF = jnp.bfloat16
F32 = jnp.float32
VMEM_BYTES = 16 * 1024 * 1024


def around(x, axis, by):
    count = lax.axis_size(axis)
    return lax.ppermute(x, axis, [(i, (i + by) % count) for i in range(count)])


def from_behind(x, axis, by):
    count = lax.axis_size(axis)
    pairs = [(i, i + by) for i in range(count) if 0 <= i + by < count]
    return lax.ppermute(x, axis, pairs)


def dot32(a, b):
    return jnp.dot(a, b, preferred_element_type=F32)


def ring_pieces(x, axis, cut, works=None):
    count = lax.axis_size(axis)
    half = count // 2
    works = works or {}
    made = {}
    parts = x if isinstance(x, list) else [x]

    moving = [(p, p) for p in parts]
    found = {0: parts}
    for step in range(1, half):
        arrived = [(around(a, axis, 1), around(b, axis, -1)) for a, b in moving]
        if step in works:
            made[step] = works[step](dict(found), made)
            arrived[0], made[step] = lax.optimization_barrier((arrived[0], made[step]))
        moving = arrived[:1] + [lax.optimization_barrier(pair) for pair in arrived[1:]]
        found[step] = [a for a, _ in moving]
        found[count - step] = [b for _, b in moving]
    if len(parts) == 2:
        last = [around(moving[0][0], axis, 1), around(moving[1][1], axis, -1)]
    else:
        (a, b), size = moving[0], x.shape[cut] // 2
        a, b = lax.slice_in_dim(a, 0, size, axis=cut), lax.slice_in_dim(b, size, 2 * size, axis=cut)
        last = [around(a, axis, 1), around(b, axis, -1)]
    last = lax.optimization_barrier(last)
    if half in works:
        made[half] = works[half](dict(found), made)
        last, made[half] = lax.optimization_barrier((last, made[half]))
    found[half] = last
    return found, made


def nearest(pieces, count, distance):
    return {k: v for k, v in pieces.items() if min(k, count - k) <= distance}


def others(pieces, some):
    return {k: v for k, v in pieces.items() if k not in some}


VM = pl.BlockSpec(memory_space=pltpu.VMEM)
SM = pl.BlockSpec(memory_space=pltpu.SMEM)
BIG = pltpu.CompilerParams(vmem_limit_bytes=VMEM_BYTES)
STEP = 256


def chunk_call(name, z, pieces, extra, outs, finish, count, weights, rows):
    behinds = list(pieces)
    flat = [p for k in behinds for p in pieces[k]]

    several = [k for k in behinds if len(pieces[k]) > 1]
    deep = pieces[behinds[0]][0].shape[1]

    def body(z, *refs):
        refs = list(refs)
        whole = refs.pop()
        took = {}
        for k in behinds:
            took[k] = [refs.pop(0) for _ in pieces[k]]
        for n, k in enumerate(several):
            at = 0
            for ref in took[k]:
                used = min(ref.shape[0], rows - at)
                whole[n, at : at + used, :] = ref[0:used, :]
                at += used
            took[k] = [whole.at[n]]
        w = [refs.pop(0) for _ in weights]
        more = [refs.pop(0) for _ in extra]

        def step(i, _):
            here = pl.ds(pl.multiple_of(i * STEP, STEP), STEP)
            chunks = [took[k][0][here, :] for k in behinds]
            dots = [0.0] * len(w)
            for k, chunk in zip(behinds, chunks):
                at = pl.multiple_of(lax.rem(z[0] + (count - k), count) * deep, deep)
                for n, ref in enumerate(w):
                    dots[n] = dots[n] + dot32(chunk, ref[pl.ds(at, deep), :])
            finish(i, here, dots, more, refs, chunks)
            return 0

        lax.fori_loop(0, rows // STEP, step, 0)

    return pl.pallas_call(
        body,
        in_specs=[SM] + [VM] * (len(flat) + len(weights) + len(extra)),
        out_specs=tuple(VM for _ in outs),
        out_shape=tuple(outs),
        scratch_shapes=[pltpu.VMEM((max(len(several), 1), rows, deep), BF)],
        compiler_params=BIG,
        name=name,
    )(z, *flat, *weights, *extra)


def first_dots(z, pieces, before, count, w_branch, w_input, rows):
    n = w_branch.shape[1]
    outs = [jax.ShapeDtypeStruct((rows, n), F32)] * 2 + [jax.ShapeDtypeStruct((rows, 1), F32)]
    final = before is not None
    if final:
        outs = outs + [jax.ShapeDtypeStruct((8, n), F32)]

    def finish(i, here, dots, more, out, chunks):
        squares = 0.0
        for chunk in chunks:
            for c in range(0, chunk.shape[1], 128):
                wide = chunk[:, c : c + 128].astype(F32)
                squares = squares + wide * wide
        squares = jnp.sum(squares, axis=1, keepdims=True)
        if final:
            dots = [d + m[here, :] for d, m in zip(dots, more)]
            squares = squares + more[2][here, :]
        out[0][here, :] = dots[0]
        out[1][here, :] = dots[1]
        out[2][here, :] = squares
        if final:
            r = lax.rsqrt(squares[STEP - 8 :] * (1.0 / 4096.0) + EPSILON)
            out[3][...] = dots[1][STEP - 8 :] * r

    return chunk_call("first_dots", z, pieces, list(before or ()), outs, finish, count, [w_branch, w_input], rows)


def one_dot(name, z, pieces, before, count, w, rows):

    def finish(i, here, dots, more, out, chunks):
        out[0][here, :] = dots[0] + more[0][here, :] if more else dots[0]

    outs = [jax.ShapeDtypeStruct((rows, w.shape[1]), F32)]
    return chunk_call(name, z, pieces, [] if before is None else [before], outs, finish, count, [w], rows)[0]


def middle(z, pieces, before, qkv, x, count, w, each):
    rows, cols = x.shape
    outs = [
        jax.ShapeDtypeStruct((rows, HD), F32),
        jax.ShapeDtypeStruct((80, rows), BF),
        jax.ShapeDtypeStruct((rows, cols), BF),
    ]

    def finish(i, here, dots, more, out, chunks):
        d = dots[0] + more[0][here, :]
        out[0][here, :] = d[:, 0:HD] + more[1][here, 0:HD]
        resid = (d[:, HD + 128 :] + more[2][here, :].astype(F32)).astype(BF)
        out[2][here, :] = resid
        wide = resid.astype(F32)
        squares = jnp.sum(wide * wide, axis=1, keepdims=True)
        kv = d[:, HD : HD + 128] + more[1][here, HD : HD + 128]
        lane = lax.broadcasted_iota(jnp.int32, kv.shape, 1)
        turned = jnp.where(lane == 2 * each, squares, kv).T
        out[1][0 : 2 * each, here] = turned[0 : 2 * each].astype(BF)
        line = turned[2 * each : 2 * each + 16]
        main = line.astype(BF).astype(F32)
        row = lax.broadcasted_iota(jnp.int32, line.shape, 0)
        low_part = jnp.broadcast_to((line - main)[0:1], line.shape)
        both = jnp.where(row == 0, main, jnp.where(row == 1, low_part, 0.0))
        out[1][2 * each : 2 * each + 16, here] = both.astype(BF)

    return chunk_call("middle", z, pieces, [before, qkv, x], outs, finish, count, [w], rows)


def last_dot(z, pieces, before, resid, count, w):
    rows = resid.shape[0]

    def finish(i, here, dots, more, out, chunks):
        out[0][here, :] = (dots[0] + more[0][here, :] + more[1][here, :].astype(F32)).astype(BF)

    outs = [jax.ShapeDtypeStruct(resid.shape, BF)]
    return chunk_call("last_dot", z, pieces, [before, resid], outs, finish, count, [w], rows)[0]


def line_products(z, pieces, count, w, part):
    behinds = list(pieces)
    cols = pieces[behinds[0]][0].shape[1]
    n = w.shape[1]

    def body(z, *refs):
        *took, w, out, out_last, lines = refs
        for k, ref in zip(behinds, took):
            at = pl.multiple_of(lax.rem(z[0] + (count - k), count) * part, part)
            for c in range(2 * count):
                first = pieces[k][1] + c * part
                lines[c, pl.ds(at, part), :] = ref[first : first + part, :].astype(F32)
        total = 0.0
        for c in range(count):
            total = total + dot32(lines[c].astype(BF), w[c * cols : (c + 1) * cols, :])
        out[:, 0:n] = total.astype(BF)
        out[:, n : n + cols] = lines[z[0]].astype(BF)
        out_last[...] = lines[z[0] + count].astype(BF)

    return pl.pallas_call(
        body,
        in_specs=[SM] + [VM] * (len(behinds) + 1),
        out_specs=(VM, VM),
        out_shape=(
            jax.ShapeDtypeStruct((part * count, n + cols), BF),
            jax.ShapeDtypeStruct((part * count, cols), BF),
        ),
        scratch_shapes=[pltpu.VMEM((2 * count, part * count, cols), F32)],
        compiler_params=BIG,
        name="line_products",
    )(z, *[pieces[k][0] for k in behinds], w)


def window(z, core, near, far, cos, sin, count, each):
    rows = cos.shape[1] // 3
    behinds = list(near)
    flat = [p for k in behinds for p in near[k] + far[k]]
    quarter = HD // 4

    def body(z, core, *refs):
        refs = list(refs)
        raw_all, kv, sent, r_out = refs[-1], refs[-4], refs[-3], refs[-2]
        cos, sin = refs[-6], refs[-5]
        for k in behinds:
            index = lax.rem(z[0] + (count - k), count)
            at = 0
            for _ in near[k] + far[k]:
                ref = refs.pop(0)
                raw_all[index, :, at : at + ref.shape[1]] = ref[...]
                at += ref.shape[1]
        for slot in range(3):
            at = slice(slot * rows, (slot + 1) * rows)
            total = jnp.zeros((1, rows), F32)
            for k in range(count):
                total = total + raw_all[k, 2 * each : 2 * each + 1, at].astype(F32)
                total = total + raw_all[k, 2 * each + 1 : 2 * each + 2, at].astype(F32)
            r = lax.rsqrt(total * (1.0 / 4096.0) + EPSILON)
            if slot == 0:
                r_out[...] = jnp.broadcast_to(r, r_out.shape)
            n = HD // 2 // each
            head = jnp.concatenate([raw_all[k, 0:each, at] for k in range(n)], axis=0).astype(F32) * r
            first, second = head[0:quarter], head[quarter : 2 * quarter]
            c, s = cos[:, at], sin[:, at]
            done = [(0, first * c - second * s), (quarter, second * c + first * s)]
            for k in range(count):
                if k >= n:
                    done.append((k * each, raw_all[k, 0:each, at].astype(F32) * r))
                done.append((HD + k * each, raw_all[k, each : 2 * each, at].astype(F32) * r))
            for start, value in done:
                value = value.astype(BF)
                kv[start : start + value.shape[0], at] = value
                to = slice(start, start + value.shape[0])

                if slot == 0:
                    @pl.when(core[0] == 0)
                    def _():
                        sent[to, 0:rows] = value
                elif slot == 1:
                    @pl.when(core[0] == 0)
                    def _():
                        sent[to, rows : 2 * rows] = value

                    @pl.when(core[0] == 1)
                    def _():
                        sent[to, 0:rows] = value
                else:
                    @pl.when(core[0] == 1)
                    def _():
                        sent[to, rows : 2 * rows] = value

    return pl.pallas_call(
        body,
        in_specs=[SM, SM] + [VM] * (len(flat) + 2),
        out_specs=(VM, VM, VM),
        out_shape=(
            jax.ShapeDtypeStruct((2 * HD, 3 * rows), BF),
            jax.ShapeDtypeStruct((2 * HD, 2 * rows), BF),
            jax.ShapeDtypeStruct((8, rows), F32),
        ),
        scratch_shapes=[pltpu.VMEM((count, 80, 3 * rows), BF)],
        compiler_params=BIG,
        name="window",
    )(z, core, *flat, cos, sin)


def make_query(q_raw, r, cos, sin):
    rows = q_raw.shape[0]

    def body(q_raw, r, cos, sin, out):
        for b in range(rows // 128):
            at = slice(b * 128, (b + 1) * 128)
            scale = jnp.broadcast_to(r[0:1, at], (128, 128)).T * (HD**-0.5)
            c, s = cos[:, at], sin[:, at]
            turn_same = jnp.concatenate([c, c], axis=0).T
            turn_other = jnp.concatenate([-s, s], axis=0).T
            head = q_raw[at, 0:128] * scale
            spun = pltpu.roll(head, HD // 4, 1)
            out[at, 0:128] = (head * turn_same + spun * turn_other).astype(BF)
            out[at, 128:256] = (q_raw[at, 128:256] * scale).astype(BF)

    return pl.pallas_call(
        body, out_shape=jax.ShapeDtypeStruct(q_raw.shape, BF), compiler_params=BIG, name="make_query"
    )(q_raw, r, cos, sin)


def attention(query, own, other, bias):
    rows = query.shape[0]
    width = WINDOW + 128

    def body(query, own, other, bias, upper, lower, kv):
        for n, (ref, slot) in enumerate(((own, 2), (other, 1), (own, 1), (other, 0), (own, 0))):
            kv[:, n * rows : (n + 1) * rows] = ref[:, slot * rows : (slot + 1) * rows]
        row = lax.broadcasted_iota(jnp.int32, (128, 128), 0)
        col = lax.broadcasted_iota(jnp.int32, (128, 128), 1)

        def block(b, out, low):
            start = pl.multiple_of(b * 128, 128)
            seen = pl.ds(start, width)
            s = dot32(query[pl.ds(start, 128), :], kv[0:HD, seen]) + bias[:, seen]
            lead = jnp.where(col > row, s[:, 0:128], -1e30)
            tail = jnp.where(col <= row, s[:, WINDOW:width], -1e30)
            s = jnp.concatenate([lead, s[:, 128:WINDOW], tail], axis=1)
            top = jnp.max(s, axis=1, keepdims=True)
            p = jnp.exp(s - top)
            total = jnp.sum(p, axis=1, keepdims=True)
            o = lax.dot_general(
                p.astype(BF), kv[HD : 2 * HD, seen], (((1,), (1,)), ((), ())), preferred_element_type=F32
            )
            out[pl.ds(pl.multiple_of(start - low, 128), 128), :] = (o / total).astype(BF)
            return 0

        for n, (out, low) in enumerate(((upper, 0), (lower, rows // 2))):
            lax.fori_loop(n * (rows // 256), (n + 1) * (rows // 256), lambda b, c: block(b, out, low), 0)

    return pl.pallas_call(
        body,
        out_shape=(jax.ShapeDtypeStruct((rows // 2, HD), BF),) * 2,
        scratch_shapes=[pltpu.VMEM((2 * HD, WINDOW + rows), BF)],
        compiler_params=BIG,
        name="attention",
    )(query, own, other, bias)


def small_expm1(y):
    near = y * (
        1.0
        + y * (1 / 2)
        * (1.0 + y * (1 / 3) * (1.0 + y * (1 / 4) * (1.0 + y * (1 / 5) * (1.0 + y * (1 / 6)
        * (1.0 + y * (1 / 7) * (1.0 + y * (1 / 8) * (1.0 + y * (1 / 9) * (1.0 + y * (1 / 10)))))))))
    )
    return jnp.where(y > -1.0, near, jnp.exp(y) - 1.0)


def scan_body(to_branch, inner, squares, halo, taps, w_rate, w_admit, rate_scale, lsb, cub, ends, ext, prior, dec, sca, lanes_in):
    rows = inner.shape[0]
    wide = lanes_in
    ext[0:8, :] = halo[...]
    seg = rows // 8
    parts = range(wide // 128)

    def scaled_in(i, _):
        here = pl.ds(pl.multiple_of(i * 128, 128), 128)
        r = lax.rsqrt(squares[here, :] * (1.0 / 4096.0) + EPSILON)
        ext[pl.ds(pl.multiple_of(i * 128 + 8, 8), 128), :] = inner[here, :] * r
        return 0

    lax.fori_loop(0, rows // 128, scaled_in, 0)

    def gates(i, _):
        here = pl.ds(pl.multiple_of(i * 128, 128), 128)
        around_here = ext[pl.ds(pl.multiple_of(i * 128, 128), 136), :]
        conv = taps[0:1, :] * around_here[8:136]
        for tap in range(1, 4):
            conv = conv + taps[tap : tap + 1, :] * around_here[8 - tap : 136 - tap]
        low = conv.astype(BF)
        rate = jax.nn.sigmoid(dot32(low, w_rate[...]))
        log_decay = rate * rate_scale[...]
        decay = jnp.exp(log_decay)
        admit = jax.nn.sigmoid(dot32(low, w_admit[...]))
        scaled = admit * conv * jnp.sqrt(-small_expm1(2.0 * log_decay))
        for n in parts:
            dec[n][here, :] = decay[:, n * 128 : (n + 1) * 128]
            sca[n][here, :] = scaled[:, n * 128 : (n + 1) * 128]
        return 0

    lax.fori_loop(0, rows // 128, gates, 0)
    c = [dec[n][pl.ds(0, 8, stride=seg), :] for n in parts]
    h = [sca[n][pl.ds(0, 8, stride=seg), :] for n in parts]
    for t in range(1, seg):
        for n in parts:
            d = dec[n][pl.ds(t, 8, stride=seg), :]
            h[n] = d * h[n] + sca[n][pl.ds(t, 8, stride=seg), :]
            c[n] = c[n] * d
            dec[n][pl.ds(t, 8, stride=seg), :] = c[n]
            sca[n][pl.ds(t, 8, stride=seg), :] = h[n]
    c, h = jnp.concatenate(c, axis=1), jnp.concatenate(h, axis=1)
    before_h = jnp.zeros((1, wide), F32)
    before_c = jnp.ones((1, wide), F32)
    befores = []
    for g in range(8):
        befores.append((before_h, before_c))
        before_h = h[g : g + 1, :] + c[g : g + 1, :] * before_h
        before_c = c[g : g + 1, :] * before_c
    prior[0:8, :] = jnp.concatenate([p[0] for p in befores], axis=0)
    prior[8:16, :] = jnp.concatenate([p[1] for p in befores], axis=0)

    def joined(g, _):
        here = pl.ds(pl.multiple_of(g * seg, seg), seg)
        r = lax.rsqrt(squares[here, :] * (1.0 / 4096.0) + EPSILON)
        branch = jax.nn.gelu(to_branch[here, :] * r)
        cum = jnp.concatenate([dec[n][here, :] for n in parts], axis=1)
        state = jnp.concatenate([sca[n][here, :] for n in parts], axis=1)
        lsb[here, :] = (state + cum * prior[pl.ds(g, 1), :]) * branch
        cub[here, :] = cum * prior[pl.ds(g + 8, 1), :] * branch
        return 0

    lax.fori_loop(0, 8, joined, 0)
    for k in range(ends.shape[0]):
        ends[k, 0:1, :] = before_c
        ends[k, 1:2, :] = before_h


def local_scan(to_branch, inner, squares, halo, taps, w_rate, w_admit, rate_scale, copies):
    rows, wide = inner.shape

    def body(*refs):
        scan_body(*refs, wide)

    return pl.pallas_call(
        body,
        out_shape=(
            jax.ShapeDtypeStruct((rows, wide), F32),
            jax.ShapeDtypeStruct((rows, wide), F32),
            jax.ShapeDtypeStruct((copies, 2, wide), F32),
        ),
        scratch_shapes=[
            pltpu.VMEM((rows + 8, wide), F32),
            pltpu.VMEM((16, wide), F32),
            [pltpu.VMEM((rows, 128), F32)] * (wide // 128),
            [pltpu.VMEM((rows, 128), F32)] * (wide // 128),
        ],
        compiler_params=pltpu.CompilerParams(vmem_limit_bytes=VMEM_BYTES),
        name="local_scan",
    )(to_branch, inner, squares, halo, taps, w_rate, w_admit, rate_scale)


def apply_carry(lsb, cub, pieces, mine):
    def body(at, lsb, cub, pieces, out):
        carry = jnp.zeros((1, lsb.shape[1]), F32)
        for k in range(pieces.shape[0]):
            fresh = pieces[k, 1:2, :] + pieces[k, 0:1, :] * carry
            carry = jnp.where(k < at[0], fresh, carry)
        out[...] = (lsb[...] + cub[...] * carry).astype(BF)

    vm = pl.BlockSpec(memory_space=pltpu.VMEM)
    return pl.pallas_call(
        body,
        in_specs=[pl.BlockSpec(memory_space=pltpu.SMEM), vm, vm, vm],
        out_specs=vm,
        out_shape=jax.ShapeDtypeStruct(lsb.shape, BF),
        compiler_params=pltpu.CompilerParams(vmem_limit_bytes=VMEM_BYTES),
        name="apply_carry",
    )(mine, lsb, cub, pieces)


def on_device(
    tokens, w_branch, w_input, conv_kernel, w_rate, w_admit, lam, w_out, w_query, w_key, w_value, w_attn_out
):
    batch, rows, cols = tokens.shape
    width = w_branch.shape[0]
    n_mp, n_ctx = lax.axis_size("mp"), lax.axis_size("ctx")
    z, j = lax.axis_index("mp"), lax.axis_index("ctx")
    z, j, core, base, first_seen, tokens = lax.optimization_barrier(
        (z, j, lax.rem(j, 2), j * rows, WINDOW - j * rows, tokens)
    )
    lru = w_branch.shape[1]
    x = tokens.reshape(rows, cols)

    zs, cores = z.reshape(1), core.reshape(1)
    half = n_mp // 2
    each = w_key.shape[1]
    part = w_out.shape[0] // n_ctx

    def lines_of(w):
        return lax.dynamic_slice_in_dim(w, j * part, part, 0)

    def along_ctx(a):
        return lax.all_gather(a, "ctx", axis=0)

    def in_order(a):
        whole = a.reshape(n_ctx, n_mp, part, a.shape[-1]).transpose(1, 0, 2, 3)
        return whole.reshape(n_mp * n_ctx * part, a.shape[-1])

    lines = jnp.stack([lines_of(w_out), lines_of(w_attn_out)]).reshape(2, part, n_mp, cols)
    lines = lines.transpose(0, 2, 1, 3).reshape(2 * n_mp * part, cols)

    tall = (rows + lines.shape[0]) // 2

    def joined_weights(found, made):
        return jnp.concatenate([w_query, w_key, w_value, jnp.zeros((width, 128 - 2 * each), BF)], axis=1)

    def tables(found, made):
        here, _ = lax.optimization_barrier((base, found[1][0]))
        span = WINDOW + rows
        freqs = 10000.0 ** (-jnp.arange(HD // 4, dtype=F32) * 2.0 / (HD // 2))
        slots = jnp.concatenate([jnp.arange(rows, dtype=jnp.int32) - back * rows for back in (0, 2, 4)])
        angles = freqs[:, None] * (here + slots).astype(F32)[None, :]
        cos_k, sin_k = jnp.cos(angles), jnp.sin(angles)
        bias = jnp.where(jnp.arange(span, dtype=jnp.int32) >= first_seen, 0.0, -1e30).astype(F32)[None]
        rate_scale = (-8.0 * jax.nn.softplus(-lam)).reshape(1, lru)
        return cos_k, sin_k, bias, rate_scale

    def first_part(found, made):
        return first_dots(zs, found, None, n_mp, w_branch, w_input, rows)

    of_x, made = ring_pieces([x[:tall], jnp.concatenate([x[tall:], lines], axis=0)], "mp", 0, {1: joined_weights, 2: tables, 3: first_part})
    w_qkv = made[1]
    cos_k, sin_k, bias, rate_scale = made[2]
    near_x = nearest(of_x, n_mp, half - 2)
    to_branch, inner, squares, tail = first_dots(zs, others(of_x, near_x), made[3], n_mp, w_branch, w_input, rows)

    with_lines = {k: (v[-1], rows - (0 if len(v) == 1 else v[0].shape[0])) for k, v in of_x.items()}
    zs_late, tail = lax.optimization_barrier((zs, tail))
    products, last_lines = line_products(zs_late, with_lines, n_mp, w_qkv, part)
    w_second = along_ctx(products)
    halo = from_behind(tail, "ctx", 1)

    lsb, cub, ends = local_scan(
        to_branch, inner, squares, halo, conv_kernel, w_rate[0], w_admit[0], rate_scale, n_ctx
    )
    last_lines, ends = lax.optimization_barrier((last_lines, ends))
    w_last = along_ctx(last_lines)
    carried = lax.all_to_all(ends, "ctx", split_axis=0, concat_axis=0, tiled=True)
    gated = apply_carry(lsb, cub, carried, j.reshape(1))

    def after(value, found):
        flat, tree = jax.tree.flatten(value)
        *flat, _ = lax.optimization_barrier((*flat, found[0][0]))
        return jax.tree.unflatten(tree, flat)

    def some_of_x(found, made):
        return one_dot("first_qkv", zs, after(near_x, found), None, n_mp, w_qkv, rows)

    def rest_of_x(found, made):
        return one_dot("first_qkv", zs, others(of_x, near_x), made[1], n_mp, w_qkv, rows)

    def second_weights(found, made):
        return in_order(after(w_second, {0: [found[1][0]]}))

    def some_second(found, made):
        return one_dot("second", zs, nearest(found, n_mp, half - 2), None, n_mp, made[3], rows)

    pieces, made = ring_pieces(
        gated, "mp", 0, {1: some_of_x, 2: rest_of_x, 3: second_weights, 4: some_second}
    )
    late = others(pieces, nearest(pieces, n_mp, half - 2))
    q_raw, block, resid = middle(zs, late, made[4], made[2], x, n_mp, made[3], each)

    def last_weights(found, made):
        return in_order(after(w_last, {0: [found[2][0]]}))

    line = jnp.concatenate([block, from_behind(block, "ctx", 2), from_behind(block, "ctx", 4)], axis=1)
    near, made = ring_pieces(line, "mp", 1, {3: last_weights})
    w_last = made[3]
    own, sent, r = window(zs, cores, near, {k: [] for k in near}, cos_k, sin_k, n_mp, each)
    other = lax.ppermute(sent, "ctx", [(i, i ^ 1) for i in range(n_ctx)])
    query = make_query(q_raw, r, cos_k, sin_k)
    attended = attention(query, own, other, bias)

    def some_last(found, made):
        return one_dot("third", zs, nearest(found, n_mp, half - 2), None, n_mp, w_last, rows)

    pieces, made = ring_pieces(list(attended), "mp", 0, {3: some_last})
    late = others(pieces, nearest(pieces, n_mp, half - 2))
    last = last_dot(zs, late, made[3], resid, n_mp, w_last)
    return last.reshape(batch, rows, cols)


def solution(mesh):
    in_specs = (
        P(None, "ctx", "mp"),
        P(None, "mp"),
        P(None, "mp"),
        P(None, "mp"),
        P("mp", None, None),
        P("mp", None, None),
        P("mp"),
        P("mp", None),
        P(None, "mp"),
        P(None, "mp"),
        P(None, "mp"),
        P("mp", None),
    )
    return jax.shard_map(
        on_device, mesh=mesh, in_specs=in_specs, out_specs=P(None, "ctx", "mp"), check_vma=False
    )
```

```python
import jax
import jax.numpy as jnp
from jax import lax
from jax.experimental import pallas as pl
from jax.experimental.pallas import tpu as pltpu
from jax.sharding import PartitionSpec as P

HD = 256
WINDOW = 2048
EPSILON = 1e-06
BF = jnp.bfloat16
F32 = jnp.float32
VMEM_BYTES = 16 * 1024 * 1024


def around(x, axis, by):
    count = lax.axis_size(axis)
    return lax.ppermute(x, axis, [(i, (i + by) % count) for i in range(count)])


def from_behind(x, axis, by):
    count = lax.axis_size(axis)
    pairs = [(i, i + by) for i in range(count) if 0 <= i + by < count]
    return lax.ppermute(x, axis, pairs)


def dot32(a, b):
    return jnp.dot(a, b, preferred_element_type=F32)


def ring_pieces(x, axis, cut, works=None):
    count = lax.axis_size(axis)
    half = count // 2
    works = works or {}
    made = {}
    parts = x if isinstance(x, list) else [x]

    moving = [(p, p) for p in parts]
    found = {0: parts}
    for step in range(1, half):
        arrived = [(around(a, axis, 1), around(b, axis, -1)) for a, b in moving]
        if step in works:
            made[step] = works[step](dict(found), made)
            arrived[0], made[step] = lax.optimization_barrier((arrived[0], made[step]))
        moving = arrived[:1] + [lax.optimization_barrier(pair) for pair in arrived[1:]]
        found[step] = [a for a, _ in moving]
        found[count - step] = [b for _, b in moving]
    if len(parts) == 2:
        last = [around(moving[0][0], axis, 1), around(moving[1][1], axis, -1)]
    else:
        (a, b), size = moving[0], x.shape[cut] // 2
        a, b = lax.slice_in_dim(a, 0, size, axis=cut), lax.slice_in_dim(b, size, 2 * size, axis=cut)
        last = [around(a, axis, 1), around(b, axis, -1)]
    last = lax.optimization_barrier(last)
    if half in works:
        made[half] = works[half](dict(found), made)
        last, made[half] = lax.optimization_barrier((last, made[half]))
    found[half] = last
    return found, made


def nearest(pieces, count, distance):
    return {k: v for k, v in pieces.items() if min(k, count - k) <= distance}


def others(pieces, some):
    return {k: v for k, v in pieces.items() if k not in some}


VM = pl.BlockSpec(memory_space=pltpu.VMEM)
SM = pl.BlockSpec(memory_space=pltpu.SMEM)
BIG = pltpu.CompilerParams(vmem_limit_bytes=VMEM_BYTES)
STEP = 256


def chunk_call(name, z, pieces, extra, outs, finish, count, weights, rows):
    behinds = list(pieces)
    flat = [p for k in behinds for p in pieces[k]]

    several = [k for k in behinds if len(pieces[k]) > 1]
    deep = pieces[behinds[0]][0].shape[1]

    def body(z, *refs):
        refs = list(refs)
        whole = refs.pop()
        took = {}
        for k in behinds:
            took[k] = [refs.pop(0) for _ in pieces[k]]
        for n, k in enumerate(several):
            at = 0
            for ref in took[k]:
                used = min(ref.shape[0], rows - at)
                whole[n, at : at + used, :] = ref[0:used, :]
                at += used
            took[k] = [whole.at[n]]
        w = [refs.pop(0) for _ in weights]
        more = [refs.pop(0) for _ in extra]

        def step(i, _):
            here = pl.ds(pl.multiple_of(i * STEP, STEP), STEP)
            chunks = [took[k][0][here, :] for k in behinds]
            dots = [0.0] * len(w)
            for k, chunk in zip(behinds, chunks):
                at = pl.multiple_of(lax.rem(z[0] + (count - k), count) * deep, deep)
                for n, ref in enumerate(w):
                    dots[n] = dots[n] + dot32(chunk, ref[pl.ds(at, deep), :])
            finish(i, here, dots, more, refs, chunks)
            return 0

        lax.fori_loop(0, rows // STEP, step, 0)

    return pl.pallas_call(
        body,
        in_specs=[SM] + [VM] * (len(flat) + len(weights) + len(extra)),
        out_specs=tuple(VM for _ in outs),
        out_shape=tuple(outs),
        scratch_shapes=[pltpu.VMEM((max(len(several), 1), rows, deep), BF)],
        compiler_params=BIG,
        name=name,
    )(z, *flat, *weights, *extra)


def first_dots(z, pieces, before, count, w_branch, w_input, rows):
    n = w_branch.shape[1]
    outs = [jax.ShapeDtypeStruct((rows, n), F32)] * 2 + [jax.ShapeDtypeStruct((rows, 1), F32)]
    final = before is not None
    if final:
        outs = outs + [jax.ShapeDtypeStruct((8, n), F32)]

    def finish(i, here, dots, more, out, chunks):
        squares = 0.0
        for chunk in chunks:
            for c in range(0, chunk.shape[1], 128):
                wide = chunk[:, c : c + 128].astype(F32)
                squares = squares + wide * wide
        squares = jnp.sum(squares, axis=1, keepdims=True)
        if final:
            dots = [d + m[here, :] for d, m in zip(dots, more)]
            squares = squares + more[2][here, :]
        out[0][here, :] = dots[0]
        out[1][here, :] = dots[1]
        out[2][here, :] = squares
        if final:
            r = lax.rsqrt(squares[STEP - 8 :] * (1.0 / 4096.0) + EPSILON)
            out[3][...] = dots[1][STEP - 8 :] * r

    return chunk_call("first_dots", z, pieces, list(before or ()), outs, finish, count, [w_branch, w_input], rows)


def one_dot(name, z, pieces, before, count, w, rows):

    def finish(i, here, dots, more, out, chunks):
        out[0][here, :] = dots[0] + more[0][here, :] if more else dots[0]

    outs = [jax.ShapeDtypeStruct((rows, w.shape[1]), F32)]
    return chunk_call(name, z, pieces, [] if before is None else [before], outs, finish, count, [w], rows)[0]


def middle(z, pieces, before, qkv, x, count, w, each):
    rows, cols = x.shape
    outs = [
        jax.ShapeDtypeStruct((rows, HD), F32),
        jax.ShapeDtypeStruct((80, rows), BF),
        jax.ShapeDtypeStruct((rows, cols), BF),
    ]

    def finish(i, here, dots, more, out, chunks):
        d = dots[0] + more[0][here, :]
        out[0][here, :] = d[:, 0:HD] + more[1][here, 0:HD]
        resid = (d[:, HD + 128 :] + more[2][here, :].astype(F32)).astype(BF)
        out[2][here, :] = resid
        wide = resid.astype(F32)
        squares = jnp.sum(wide * wide, axis=1, keepdims=True)
        kv = d[:, HD : HD + 128] + more[1][here, HD : HD + 128]
        lane = lax.broadcasted_iota(jnp.int32, kv.shape, 1)
        turned = jnp.where(lane == 2 * each, squares, kv).T
        out[1][0 : 2 * each, here] = turned[0 : 2 * each].astype(BF)
        line = turned[2 * each : 2 * each + 16]
        main = line.astype(BF).astype(F32)
        row = lax.broadcasted_iota(jnp.int32, line.shape, 0)
        low_part = jnp.broadcast_to((line - main)[0:1], line.shape)
        both = jnp.where(row == 0, main, jnp.where(row == 1, low_part, 0.0))
        out[1][2 * each : 2 * each + 16, here] = both.astype(BF)

    return chunk_call("middle", z, pieces, [before, qkv, x], outs, finish, count, [w], rows)


def last_dot(z, pieces, before, resid, count, w):
    rows = resid.shape[0]

    def finish(i, here, dots, more, out, chunks):
        out[0][here, :] = (dots[0] + more[0][here, :] + more[1][here, :].astype(F32)).astype(BF)

    outs = [jax.ShapeDtypeStruct(resid.shape, BF)]
    return chunk_call("last_dot", z, pieces, [before, resid], outs, finish, count, [w], rows)[0]


def line_products(z, pieces, count, w, part):
    behinds = list(pieces)
    cols = pieces[behinds[0]][0].shape[1]
    n = w.shape[1]

    def body(z, *refs):
        *took, w, out, out_last, lines = refs
        for k, ref in zip(behinds, took):
            at = pl.multiple_of(lax.rem(z[0] + (count - k), count) * part, part)
            for c in range(2 * count):
                first = pieces[k][1] + c * part
                lines[c, pl.ds(at, part), :] = ref[first : first + part, :].astype(F32)
        total = 0.0
        for c in range(count):
            total = total + dot32(lines[c].astype(BF), w[c * cols : (c + 1) * cols, :])
        out[:, 0:n] = total.astype(BF)
        out[:, n : n + cols] = lines[z[0]].astype(BF)
        out_last[...] = lines[z[0] + count].astype(BF)

    return pl.pallas_call(
        body,
        in_specs=[SM] + [VM] * (len(behinds) + 1),
        out_specs=(VM, VM),
        out_shape=(
            jax.ShapeDtypeStruct((part * count, n + cols), BF),
            jax.ShapeDtypeStruct((part * count, cols), BF),
        ),
        scratch_shapes=[pltpu.VMEM((2 * count, part * count, cols), F32)],
        compiler_params=BIG,
        name="line_products",
    )(z, *[pieces[k][0] for k in behinds], w)


def window(z, core, near, far, cos, sin, count, each):
    rows = cos.shape[1] // 3
    behinds = list(near)
    flat = [p for k in behinds for p in near[k] + far[k]]
    quarter = HD // 4

    def body(z, core, *refs):
        refs = list(refs)
        raw_all, kv, sent, r_out = refs[-1], refs[-4], refs[-3], refs[-2]
        cos, sin = refs[-6], refs[-5]
        for k in behinds:
            index = lax.rem(z[0] + (count - k), count)
            at = 0
            for _ in near[k] + far[k]:
                ref = refs.pop(0)
                raw_all[index, :, at : at + ref.shape[1]] = ref[...]
                at += ref.shape[1]
        for slot in range(3):
            at = slice(slot * rows, (slot + 1) * rows)
            total = jnp.zeros((1, rows), F32)
            for k in range(count):
                total = total + raw_all[k, 2 * each : 2 * each + 1, at].astype(F32)
                total = total + raw_all[k, 2 * each + 1 : 2 * each + 2, at].astype(F32)
            r = lax.rsqrt(total * (1.0 / 4096.0) + EPSILON)
            if slot == 0:
                r_out[...] = jnp.broadcast_to(r, r_out.shape)
            n = HD // 2 // each
            head = jnp.concatenate([raw_all[k, 0:each, at] for k in range(n)], axis=0).astype(F32) * r
            first, second = head[0:quarter], head[quarter : 2 * quarter]
            c, s = cos[:, at], sin[:, at]
            done = [(0, first * c - second * s), (quarter, second * c + first * s)]
            for k in range(count):
                if k >= n:
                    done.append((k * each, raw_all[k, 0:each, at].astype(F32) * r))
                done.append((HD + k * each, raw_all[k, each : 2 * each, at].astype(F32) * r))
            for start, value in done:
                value = value.astype(BF)
                kv[start : start + value.shape[0], at] = value
                to = slice(start, start + value.shape[0])

                if slot == 0:
                    @pl.when(core[0] == 0)
                    def _():
                        sent[to, 0:rows] = value
                elif slot == 1:
                    @pl.when(core[0] == 0)
                    def _():
                        sent[to, rows : 2 * rows] = value

                    @pl.when(core[0] == 1)
                    def _():
                        sent[to, 0:rows] = value
                else:
                    @pl.when(core[0] == 1)
                    def _():
                        sent[to, rows : 2 * rows] = value

    return pl.pallas_call(
        body,
        in_specs=[SM, SM] + [VM] * (len(flat) + 2),
        out_specs=(VM, VM, VM),
        out_shape=(
            jax.ShapeDtypeStruct((2 * HD, 3 * rows), BF),
            jax.ShapeDtypeStruct((2 * HD, 2 * rows), BF),
            jax.ShapeDtypeStruct((8, rows), F32),
        ),
        scratch_shapes=[pltpu.VMEM((count, 80, 3 * rows), BF)],
        compiler_params=BIG,
        name="window",
    )(z, core, *flat, cos, sin)


def make_query(q_raw, r, cos, sin):
    rows = q_raw.shape[0]

    def body(q_raw, r, cos, sin, out):
        for b in range(rows // 128):
            at = slice(b * 128, (b + 1) * 128)
            scale = jnp.broadcast_to(r[0:1, at], (128, 128)).T * (HD**-0.5)
            c, s = cos[:, at], sin[:, at]
            turn_same = jnp.concatenate([c, c], axis=0).T
            turn_other = jnp.concatenate([-s, s], axis=0).T
            head = q_raw[at, 0:128] * scale
            spun = pltpu.roll(head, HD // 4, 1)
            out[at, 0:128] = (head * turn_same + spun * turn_other).astype(BF)
            out[at, 128:256] = (q_raw[at, 128:256] * scale).astype(BF)

    return pl.pallas_call(
        body, out_shape=jax.ShapeDtypeStruct(q_raw.shape, BF), compiler_params=BIG, name="make_query"
    )(q_raw, r, cos, sin)


def attention(query, own, other, bias):
    rows = query.shape[0]
    width = WINDOW + 128

    def body(query, own, other, bias, upper, lower, kv):
        for n, (ref, slot) in enumerate(((own, 2), (other, 1), (own, 1), (other, 0), (own, 0))):
            kv[:, n * rows : (n + 1) * rows] = ref[:, slot * rows : (slot + 1) * rows]
        row = lax.broadcasted_iota(jnp.int32, (128, 128), 0)
        col = lax.broadcasted_iota(jnp.int32, (128, 128), 1)

        def block(b, out, low):
            start = pl.multiple_of(b * 128, 128)
            seen = pl.ds(start, width)
            s = dot32(query[pl.ds(start, 128), :], kv[0:HD, seen]) + bias[:, seen]
            lead = jnp.where(col > row, s[:, 0:128], -1e30)
            tail = jnp.where(col <= row, s[:, WINDOW:width], -1e30)
            s = jnp.concatenate([lead, s[:, 128:WINDOW], tail], axis=1)
            top = jnp.max(s, axis=1, keepdims=True)
            p = jnp.exp(s - top)
            total = jnp.sum(p, axis=1, keepdims=True)
            o = lax.dot_general(
                p.astype(BF), kv[HD : 2 * HD, seen], (((1,), (1,)), ((), ())), preferred_element_type=F32
            )
            out[pl.ds(pl.multiple_of(start - low, 128), 128), :] = (o / total).astype(BF)
            return 0

        for n, (out, low) in enumerate(((upper, 0), (lower, rows // 2))):
            lax.fori_loop(n * (rows // 256), (n + 1) * (rows // 256), lambda b, c: block(b, out, low), 0)

    return pl.pallas_call(
        body,
        out_shape=(jax.ShapeDtypeStruct((rows // 2, HD), BF),) * 2,
        scratch_shapes=[pltpu.VMEM((2 * HD, WINDOW + rows), BF)],
        compiler_params=BIG,
        name="attention",
    )(query, own, other, bias)


def small_expm1(y):
    near = y * (
        1.0
        + y * (1 / 2)
        * (1.0 + y * (1 / 3) * (1.0 + y * (1 / 4) * (1.0 + y * (1 / 5) * (1.0 + y * (1 / 6)
        * (1.0 + y * (1 / 7) * (1.0 + y * (1 / 8) * (1.0 + y * (1 / 9) * (1.0 + y * (1 / 10)))))))))
    )
    return jnp.where(y > -1.0, near, jnp.exp(y) - 1.0)


def scan_body(to_branch, inner, squares, halo, taps, w_rate, w_admit, rate_scale, lsb, cub, ends, ext, prior, dec, sca, lanes_in):
    rows = inner.shape[0]
    wide = lanes_in
    ext[0:8, :] = halo[...]
    seg = rows // 8
    parts = range(wide // 128)

    def scaled_in(i, _):
        here = pl.ds(pl.multiple_of(i * 128, 128), 128)
        r = lax.rsqrt(squares[here, :] * (1.0 / 4096.0) + EPSILON)
        ext[pl.ds(pl.multiple_of(i * 128 + 8, 8), 128), :] = inner[here, :] * r
        return 0

    lax.fori_loop(0, rows // 128, scaled_in, 0)

    def gates(i, _):
        here = pl.ds(pl.multiple_of(i * 128, 128), 128)
        around_here = ext[pl.ds(pl.multiple_of(i * 128, 128), 136), :]
        conv = taps[0:1, :] * around_here[8:136]
        for tap in range(1, 4):
            conv = conv + taps[tap : tap + 1, :] * around_here[8 - tap : 136 - tap]
        low = conv.astype(BF)
        rate = jax.nn.sigmoid(dot32(low, w_rate[...]))
        log_decay = rate * rate_scale[...]
        decay = jnp.exp(log_decay)
        admit = jax.nn.sigmoid(dot32(low, w_admit[...]))
        scaled = admit * conv * jnp.sqrt(-small_expm1(2.0 * log_decay))
        for n in parts:
            dec[n][here, :] = decay[:, n * 128 : (n + 1) * 128]
            sca[n][here, :] = scaled[:, n * 128 : (n + 1) * 128]
        return 0

    lax.fori_loop(0, rows // 128, gates, 0)
    c = [dec[n][pl.ds(0, 8, stride=seg), :] for n in parts]
    h = [sca[n][pl.ds(0, 8, stride=seg), :] for n in parts]
    for t in range(1, seg):
        for n in parts:
            d = dec[n][pl.ds(t, 8, stride=seg), :]
            h[n] = d * h[n] + sca[n][pl.ds(t, 8, stride=seg), :]
            c[n] = c[n] * d
            dec[n][pl.ds(t, 8, stride=seg), :] = c[n]
            sca[n][pl.ds(t, 8, stride=seg), :] = h[n]
    c, h = jnp.concatenate(c, axis=1), jnp.concatenate(h, axis=1)
    before_h = jnp.zeros((1, wide), F32)
    before_c = jnp.ones((1, wide), F32)
    befores = []
    for g in range(8):
        befores.append((before_h, before_c))
        before_h = h[g : g + 1, :] + c[g : g + 1, :] * before_h
        before_c = c[g : g + 1, :] * before_c
    prior[0:8, :] = jnp.concatenate([p[0] for p in befores], axis=0)
    prior[8:16, :] = jnp.concatenate([p[1] for p in befores], axis=0)

    def joined(g, _):
        here = pl.ds(pl.multiple_of(g * seg, seg), seg)
        r = lax.rsqrt(squares[here, :] * (1.0 / 4096.0) + EPSILON)
        branch = jax.nn.gelu(to_branch[here, :] * r)
        cum = jnp.concatenate([dec[n][here, :] for n in parts], axis=1)
        state = jnp.concatenate([sca[n][here, :] for n in parts], axis=1)
        lsb[here, :] = (state + cum * prior[pl.ds(g, 1), :]) * branch
        cub[here, :] = cum * prior[pl.ds(g + 8, 1), :] * branch
        return 0

    lax.fori_loop(0, 8, joined, 0)
    for k in range(ends.shape[0]):
        ends[k, 0:1, :] = before_c
        ends[k, 1:2, :] = before_h


def local_scan(to_branch, inner, squares, halo, taps, w_rate, w_admit, rate_scale, copies):
    rows, wide = inner.shape

    def body(*refs):
        scan_body(*refs, wide)

    return pl.pallas_call(
        body,
        out_shape=(
            jax.ShapeDtypeStruct((rows, wide), F32),
            jax.ShapeDtypeStruct((rows, wide), F32),
            jax.ShapeDtypeStruct((copies, 2, wide), F32),
        ),
        scratch_shapes=[
            pltpu.VMEM((rows + 8, wide), F32),
            pltpu.VMEM((16, wide), F32),
            [pltpu.VMEM((rows, 128), F32)] * (wide // 128),
            [pltpu.VMEM((rows, 128), F32)] * (wide // 128),
        ],
        compiler_params=pltpu.CompilerParams(vmem_limit_bytes=VMEM_BYTES),
        name="local_scan",
    )(to_branch, inner, squares, halo, taps, w_rate, w_admit, rate_scale)


def apply_carry(lsb, cub, pieces, mine):
    def body(at, lsb, cub, pieces, out):
        carry = jnp.zeros((1, lsb.shape[1]), F32)
        for k in range(pieces.shape[0]):
            fresh = pieces[k, 1:2, :] + pieces[k, 0:1, :] * carry
            carry = jnp.where(k < at[0], fresh, carry)
        out[...] = (lsb[...] + cub[...] * carry).astype(BF)

    vm = pl.BlockSpec(memory_space=pltpu.VMEM)
    return pl.pallas_call(
        body,
        in_specs=[pl.BlockSpec(memory_space=pltpu.SMEM), vm, vm, vm],
        out_specs=vm,
        out_shape=jax.ShapeDtypeStruct(lsb.shape, BF),
        compiler_params=pltpu.CompilerParams(vmem_limit_bytes=VMEM_BYTES),
        name="apply_carry",
    )(mine, lsb, cub, pieces)


def on_device(
    tokens, w_branch, w_input, conv_kernel, w_rate, w_admit, lam, w_out, w_query, w_key, w_value, w_attn_out
):
    batch, rows, cols = tokens.shape
    width = w_branch.shape[0]
    n_mp, n_ctx = lax.axis_size("mp"), lax.axis_size("ctx")
    z, j = lax.axis_index("mp"), lax.axis_index("ctx")
    z, j, core, base, first_seen, tokens = lax.optimization_barrier(
        (z, j, lax.rem(j, 2), j * rows, WINDOW - j * rows, tokens)
    )
    lru = w_branch.shape[1]
    x = tokens.reshape(rows, cols)

    zs, cores = z.reshape(1), core.reshape(1)
    half = n_mp // 2
    each = w_key.shape[1]
    part = w_out.shape[0] // n_ctx

    def lines_of(w):
        return lax.dynamic_slice_in_dim(w, j * part, part, 0)

    def along_ctx(a):
        return lax.all_gather(a, "ctx", axis=0)

    def in_order(a):
        whole = a.reshape(n_ctx, n_mp, part, a.shape[-1]).transpose(1, 0, 2, 3)
        return whole.reshape(n_mp * n_ctx * part, a.shape[-1])

    lines = jnp.stack([lines_of(w_out), lines_of(w_attn_out)]).reshape(2, part, n_mp, cols)
    lines = lines.transpose(0, 2, 1, 3).reshape(2 * n_mp * part, cols)

    tall = (rows + lines.shape[0]) // 2

    def joined_weights(found, made):
        return jnp.concatenate([w_query, w_key, w_value, jnp.zeros((width, 128 - 2 * each), BF)], axis=1)

    def tables(found, made):
        here, _ = lax.optimization_barrier((base, found[1][0]))
        span = WINDOW + rows
        freqs = 10000.0 ** (-jnp.arange(HD // 4, dtype=F32) * 2.0 / (HD // 2))
        slots = jnp.concatenate([jnp.arange(rows, dtype=jnp.int32) - back * rows for back in (0, 2, 4)])
        angles = freqs[:, None] * (here + slots).astype(F32)[None, :]
        cos_k, sin_k = jnp.cos(angles), jnp.sin(angles)
        bias = jnp.where(jnp.arange(span, dtype=jnp.int32) >= first_seen, 0.0, -1e30).astype(F32)[None]
        rate_scale = (-8.0 * jax.nn.softplus(-lam)).reshape(1, lru)
        return cos_k, sin_k, bias, rate_scale

    def first_part(found, made):
        return first_dots(zs, found, None, n_mp, w_branch, w_input, rows)

    of_x, made = ring_pieces([x[:tall], jnp.concatenate([x[tall:], lines], axis=0)], "mp", 0, {1: joined_weights, 2: tables, 3: first_part})
    w_qkv = made[1]
    cos_k, sin_k, bias, rate_scale = made[2]
    near_x = nearest(of_x, n_mp, half - 2)
    to_branch, inner, squares, tail = first_dots(zs, others(of_x, near_x), made[3], n_mp, w_branch, w_input, rows)

    with_lines = {k: (v[-1], rows - (0 if len(v) == 1 else v[0].shape[0])) for k, v in of_x.items()}
    zs_late, tail = lax.optimization_barrier((zs, tail))
    products, last_lines = line_products(zs_late, with_lines, n_mp, w_qkv, part)
    w_second = along_ctx(products)
    halo = from_behind(tail, "ctx", 1)

    lsb, cub, ends = local_scan(
        to_branch, inner, squares, halo, conv_kernel, w_rate[0], w_admit[0], rate_scale, n_ctx
    )
    carried = lax.all_to_all(ends, "ctx", split_axis=0, concat_axis=0, tiled=True)
    gated = apply_carry(lsb, cub, carried, j.reshape(1))
    last_lines, gated = lax.optimization_barrier((last_lines, gated))
    w_last = along_ctx(last_lines)

    def after(value, found):
        flat, tree = jax.tree.flatten(value)
        *flat, _ = lax.optimization_barrier((*flat, found[0][0]))
        return jax.tree.unflatten(tree, flat)

    def some_of_x(found, made):
        return one_dot("first_qkv", zs, after(near_x, found), None, n_mp, w_qkv, rows)

    def rest_of_x(found, made):
        return one_dot("first_qkv", zs, others(of_x, near_x), made[1], n_mp, w_qkv, rows)

    def second_weights(found, made):
        return in_order(after(w_second, {0: [found[1][0]]}))

    def some_second(found, made):
        return one_dot("second", zs, nearest(found, n_mp, half - 2), None, n_mp, made[3], rows)

    pieces, made = ring_pieces(
        gated, "mp", 0, {1: some_of_x, 2: rest_of_x, 3: second_weights, 4: some_second}
    )
    late = others(pieces, nearest(pieces, n_mp, half - 2))
    q_raw, block, resid = middle(zs, late, made[4], made[2], x, n_mp, made[3], each)

    def last_weights(found, made):
        return in_order(after(w_last, {0: [found[2][0]]}))

    line = jnp.concatenate([block, from_behind(block, "ctx", 2), from_behind(block, "ctx", 4)], axis=1)
    near, made = ring_pieces(line, "mp", 1, {3: last_weights})
    w_last = made[3]
    own, sent, r = window(zs, cores, near, {k: [] for k in near}, cos_k, sin_k, n_mp, each)
    other = lax.ppermute(sent, "ctx", [(i, i ^ 1) for i in range(n_ctx)])
    query = make_query(q_raw, r, cos_k, sin_k)
    attended = attention(query, own, other, bias)

    def some_last(found, made):
        return one_dot("third", zs, nearest(found, n_mp, half - 2), None, n_mp, w_last, rows)

    pieces, made = ring_pieces(list(attended), "mp", 0, {3: some_last})
    late = others(pieces, nearest(pieces, n_mp, half - 2))
    last = last_dot(zs, late, made[3], resid, n_mp, w_last)
    return last.reshape(batch, rows, cols)


def solution(mesh):
    in_specs = (
        P(None, "ctx", "mp"),
        P(None, "mp"),
        P(None, "mp"),
        P(None, "mp"),
        P("mp", None, None),
        P("mp", None, None),
        P("mp"),
        P("mp", None),
        P(None, "mp"),
        P(None, "mp"),
        P(None, "mp"),
        P("mp", None),
    )
    return jax.shard_map(
        on_device, mesh=mesh, in_specs=in_specs, out_specs=P(None, "ctx", "mp"), check_vma=False
    )
```

```python
import jax
import jax.numpy as jnp
from jax import lax
from jax.experimental import pallas as pl
from jax.experimental.pallas import tpu as pltpu
from jax.sharding import PartitionSpec as P

HD = 256
WINDOW = 2048
EPSILON = 1e-06
BF = jnp.bfloat16
F32 = jnp.float32
VMEM_BYTES = 16 * 1024 * 1024


def around(x, axis, by):
    count = lax.axis_size(axis)
    return lax.ppermute(x, axis, [(i, (i + by) % count) for i in range(count)])


def from_behind(x, axis, by):
    count = lax.axis_size(axis)
    pairs = [(i, i + by) for i in range(count) if 0 <= i + by < count]
    return lax.ppermute(x, axis, pairs)


def dot32(a, b):
    return jnp.dot(a, b, preferred_element_type=F32)


def ring_pieces(x, axis, cut, works=None):
    count = lax.axis_size(axis)
    half = count // 2
    works = works or {}
    made = {}
    parts = x if isinstance(x, list) else [x]

    moving = [(p, p) for p in parts]
    found = {0: parts}
    for step in range(1, half):
        arrived = [(around(a, axis, 1), around(b, axis, -1)) for a, b in moving]
        if step in works:
            made[step] = works[step](dict(found), made)
            arrived[0], made[step] = lax.optimization_barrier((arrived[0], made[step]))
        moving = arrived[:1] + [lax.optimization_barrier(pair) for pair in arrived[1:]]
        found[step] = [a for a, _ in moving]
        found[count - step] = [b for _, b in moving]
    if len(parts) == 2:
        last = [around(moving[0][0], axis, 1), around(moving[1][1], axis, -1)]
    else:
        (a, b), size = moving[0], x.shape[cut] // 2
        a, b = lax.slice_in_dim(a, 0, size, axis=cut), lax.slice_in_dim(b, size, 2 * size, axis=cut)
        last = [around(a, axis, 1), around(b, axis, -1)]
    last = lax.optimization_barrier(last)
    if half in works:
        made[half] = works[half](dict(found), made)
        last, made[half] = lax.optimization_barrier((last, made[half]))
    found[half] = last
    return found, made


def nearest(pieces, count, distance):
    return {k: v for k, v in pieces.items() if min(k, count - k) <= distance}


def others(pieces, some):
    return {k: v for k, v in pieces.items() if k not in some}


VM = pl.BlockSpec(memory_space=pltpu.VMEM)
SM = pl.BlockSpec(memory_space=pltpu.SMEM)
BIG = pltpu.CompilerParams(vmem_limit_bytes=VMEM_BYTES)
STEP = 512


def chunk_call(name, z, pieces, extra, outs, finish, count, weights, rows):
    behinds = list(pieces)
    flat = [p for k in behinds for p in pieces[k]]

    several = [k for k in behinds if len(pieces[k]) > 1]
    deep = pieces[behinds[0]][0].shape[1]

    def body(z, *refs):
        refs = list(refs)
        whole = refs.pop()
        took = {}
        for k in behinds:
            took[k] = [refs.pop(0) for _ in pieces[k]]
        for n, k in enumerate(several):
            at = 0
            for ref in took[k]:
                used = min(ref.shape[0], rows - at)
                whole[n, at : at + used, :] = ref[0:used, :]
                at += used
            took[k] = [whole.at[n]]
        w = [refs.pop(0) for _ in weights]
        more = [refs.pop(0) for _ in extra]

        def step(i, _):
            here = pl.ds(pl.multiple_of(i * STEP, STEP), STEP)
            chunks = [took[k][0][here, :] for k in behinds]
            dots = [0.0] * len(w)
            for k, chunk in zip(behinds, chunks):
                at = pl.multiple_of(lax.rem(z[0] + (count - k), count) * deep, deep)
                for n, ref in enumerate(w):
                    dots[n] = dots[n] + dot32(chunk, ref[pl.ds(at, deep), :])
            finish(i, here, dots, more, refs, chunks)
            return 0

        lax.fori_loop(0, rows // STEP, step, 0)

    return pl.pallas_call(
        body,
        in_specs=[SM] + [VM] * (len(flat) + len(weights) + len(extra)),
        out_specs=tuple(VM for _ in outs),
        out_shape=tuple(outs),
        scratch_shapes=[pltpu.VMEM((max(len(several), 1), rows, deep), BF)],
        compiler_params=BIG,
        name=name,
    )(z, *flat, *weights, *extra)


def first_dots(z, pieces, before, count, w_branch, w_input, rows):
    n = w_branch.shape[1]
    outs = [jax.ShapeDtypeStruct((rows, n), F32)] * 2 + [jax.ShapeDtypeStruct((rows, 1), F32)]
    final = before is not None
    if final:
        outs = outs + [jax.ShapeDtypeStruct((8, n), F32)]

    def finish(i, here, dots, more, out, chunks):
        squares = 0.0
        for chunk in chunks:
            for c in range(0, chunk.shape[1], 128):
                wide = chunk[:, c : c + 128].astype(F32)
                squares = squares + wide * wide
        squares = jnp.sum(squares, axis=1, keepdims=True)
        if final:
            dots = [d + m[here, :] for d, m in zip(dots, more)]
            squares = squares + more[2][here, :]
        out[0][here, :] = dots[0]
        out[1][here, :] = dots[1]
        out[2][here, :] = squares
        if final:
            r = lax.rsqrt(squares[STEP - 8 :] * (1.0 / 4096.0) + EPSILON)
            out[3][...] = dots[1][STEP - 8 :] * r

    return chunk_call("first_dots", z, pieces, list(before or ()), outs, finish, count, [w_branch, w_input], rows)


def one_dot(name, z, pieces, before, count, w, rows):

    def finish(i, here, dots, more, out, chunks):
        out[0][here, :] = dots[0] + more[0][here, :] if more else dots[0]

    outs = [jax.ShapeDtypeStruct((rows, w.shape[1]), F32)]
    return chunk_call(name, z, pieces, [] if before is None else [before], outs, finish, count, [w], rows)[0]


def middle(z, pieces, before, qkv, x, count, w, each):
    rows, cols = x.shape
    outs = [
        jax.ShapeDtypeStruct((rows, HD), F32),
        jax.ShapeDtypeStruct((80, rows), BF),
        jax.ShapeDtypeStruct((rows, cols), BF),
    ]

    def finish(i, here, dots, more, out, chunks):
        d = dots[0] + more[0][here, :]
        out[0][here, :] = d[:, 0:HD] + more[1][here, 0:HD]
        resid = (d[:, HD + 128 :] + more[2][here, :].astype(F32)).astype(BF)
        out[2][here, :] = resid
        wide = resid.astype(F32)
        squares = jnp.sum(wide * wide, axis=1, keepdims=True)
        kv = d[:, HD : HD + 128] + more[1][here, HD : HD + 128]
        lane = lax.broadcasted_iota(jnp.int32, kv.shape, 1)
        turned = jnp.where(lane == 2 * each, squares, kv).T
        out[1][0 : 2 * each, here] = turned[0 : 2 * each].astype(BF)
        line = turned[2 * each : 2 * each + 16]
        main = line.astype(BF).astype(F32)
        row = lax.broadcasted_iota(jnp.int32, line.shape, 0)
        low_part = jnp.broadcast_to((line - main)[0:1], line.shape)
        both = jnp.where(row == 0, main, jnp.where(row == 1, low_part, 0.0))
        out[1][2 * each : 2 * each + 16, here] = both.astype(BF)

    return chunk_call("middle", z, pieces, [before, qkv, x], outs, finish, count, [w], rows)


def last_dot(z, pieces, before, resid, count, w):
    rows = resid.shape[0]

    def finish(i, here, dots, more, out, chunks):
        out[0][here, :] = (dots[0] + more[0][here, :] + more[1][here, :].astype(F32)).astype(BF)

    outs = [jax.ShapeDtypeStruct(resid.shape, BF)]
    return chunk_call("last_dot", z, pieces, [before, resid], outs, finish, count, [w], rows)[0]


def line_products(z, pieces, count, w, part):
    behinds = list(pieces)
    cols = pieces[behinds[0]][0].shape[1]
    n = w.shape[1]

    def body(z, *refs):
        *took, w, out, out_last, lines = refs
        for k, ref in zip(behinds, took):
            at = pl.multiple_of(lax.rem(z[0] + (count - k), count) * part, part)
            for c in range(2 * count):
                first = pieces[k][1] + c * part
                lines[c, pl.ds(at, part), :] = ref[first : first + part, :].astype(F32)
        total = 0.0
        for c in range(count):
            total = total + dot32(lines[c].astype(BF), w[c * cols : (c + 1) * cols, :])
        out[:, 0:n] = total.astype(BF)
        out[:, n : n + cols] = lines[z[0]].astype(BF)
        out_last[...] = lines[z[0] + count].astype(BF)

    return pl.pallas_call(
        body,
        in_specs=[SM] + [VM] * (len(behinds) + 1),
        out_specs=(VM, VM),
        out_shape=(
            jax.ShapeDtypeStruct((part * count, n + cols), BF),
            jax.ShapeDtypeStruct((part * count, cols), BF),
        ),
        scratch_shapes=[pltpu.VMEM((2 * count, part * count, cols), F32)],
        compiler_params=BIG,
        name="line_products",
    )(z, *[pieces[k][0] for k in behinds], w)


def window(z, core, near, far, cos, sin, count, each):
    rows = cos.shape[1] // 3
    behinds = list(near)
    flat = [p for k in behinds for p in near[k] + far[k]]
    quarter = HD // 4

    def body(z, core, *refs):
        refs = list(refs)
        raw_all, kv, sent, r_out = refs[-1], refs[-4], refs[-3], refs[-2]
        cos, sin = refs[-6], refs[-5]
        for k in behinds:
            index = lax.rem(z[0] + (count - k), count)
            at = 0
            for _ in near[k] + far[k]:
                ref = refs.pop(0)
                raw_all[index, :, at : at + ref.shape[1]] = ref[...]
                at += ref.shape[1]
        for slot in range(3):
            at = slice(slot * rows, (slot + 1) * rows)
            total = jnp.zeros((1, rows), F32)
            for k in range(count):
                total = total + raw_all[k, 2 * each : 2 * each + 1, at].astype(F32)
                total = total + raw_all[k, 2 * each + 1 : 2 * each + 2, at].astype(F32)
            r = lax.rsqrt(total * (1.0 / 4096.0) + EPSILON)
            if slot == 0:
                r_out[...] = jnp.broadcast_to(r, r_out.shape)
            n = HD // 2 // each
            head = jnp.concatenate([raw_all[k, 0:each, at] for k in range(n)], axis=0).astype(F32) * r
            first, second = head[0:quarter], head[quarter : 2 * quarter]
            c, s = cos[:, at], sin[:, at]
            done = [(0, first * c - second * s), (quarter, second * c + first * s)]
            for k in range(count):
                if k >= n:
                    done.append((k * each, raw_all[k, 0:each, at].astype(F32) * r))
                done.append((HD + k * each, raw_all[k, each : 2 * each, at].astype(F32) * r))
            for start, value in done:
                value = value.astype(BF)
                kv[start : start + value.shape[0], at] = value
                to = slice(start, start + value.shape[0])

                if slot == 0:
                    @pl.when(core[0] == 0)
                    def _():
                        sent[to, 0:rows] = value
                elif slot == 1:
                    @pl.when(core[0] == 0)
                    def _():
                        sent[to, rows : 2 * rows] = value

                    @pl.when(core[0] == 1)
                    def _():
                        sent[to, 0:rows] = value
                else:
                    @pl.when(core[0] == 1)
                    def _():
                        sent[to, rows : 2 * rows] = value

    return pl.pallas_call(
        body,
        in_specs=[SM, SM] + [VM] * (len(flat) + 2),
        out_specs=(VM, VM, VM),
        out_shape=(
            jax.ShapeDtypeStruct((2 * HD, 3 * rows), BF),
            jax.ShapeDtypeStruct((2 * HD, 2 * rows), BF),
            jax.ShapeDtypeStruct((8, rows), F32),
        ),
        scratch_shapes=[pltpu.VMEM((count, 80, 3 * rows), BF)],
        compiler_params=BIG,
        name="window",
    )(z, core, *flat, cos, sin)


def make_query(q_raw, r, cos, sin):
    rows = q_raw.shape[0]

    def body(q_raw, r, cos, sin, out):
        for b in range(rows // 128):
            at = slice(b * 128, (b + 1) * 128)
            scale = jnp.broadcast_to(r[0:1, at], (128, 128)).T * (HD**-0.5)
            c, s = cos[:, at], sin[:, at]
            turn_same = jnp.concatenate([c, c], axis=0).T
            turn_other = jnp.concatenate([-s, s], axis=0).T
            head = q_raw[at, 0:128] * scale
            spun = pltpu.roll(head, HD // 4, 1)
            out[at, 0:128] = (head * turn_same + spun * turn_other).astype(BF)
            out[at, 128:256] = (q_raw[at, 128:256] * scale).astype(BF)

    return pl.pallas_call(
        body, out_shape=jax.ShapeDtypeStruct(q_raw.shape, BF), compiler_params=BIG, name="make_query"
    )(q_raw, r, cos, sin)


def attention(query, own, other, bias):
    rows = query.shape[0]
    width = WINDOW + 128

    def body(query, own, other, bias, upper, lower, kv):
        for n, (ref, slot) in enumerate(((own, 2), (other, 1), (own, 1), (other, 0), (own, 0))):
            kv[:, n * rows : (n + 1) * rows] = ref[:, slot * rows : (slot + 1) * rows]
        row = lax.broadcasted_iota(jnp.int32, (128, 128), 0)
        col = lax.broadcasted_iota(jnp.int32, (128, 128), 1)

        def block(b, out, low):
            start = pl.multiple_of(b * 128, 128)
            seen = pl.ds(start, width)
            s = dot32(query[pl.ds(start, 128), :], kv[0:HD, seen]) + bias[:, seen]
            lead = jnp.where(col > row, s[:, 0:128], -1e30)
            tail = jnp.where(col <= row, s[:, WINDOW:width], -1e30)
            s = jnp.concatenate([lead, s[:, 128:WINDOW], tail], axis=1)
            top = jnp.max(s, axis=1, keepdims=True)
            p = jnp.exp(s - top)
            total = jnp.sum(p, axis=1, keepdims=True)
            o = lax.dot_general(
                p.astype(BF), kv[HD : 2 * HD, seen], (((1,), (1,)), ((), ())), preferred_element_type=F32
            )
            out[pl.ds(pl.multiple_of(start - low, 128), 128), :] = (o / total).astype(BF)
            return 0

        for n, (out, low) in enumerate(((upper, 0), (lower, rows // 2))):
            lax.fori_loop(n * (rows // 256), (n + 1) * (rows // 256), lambda b, c: block(b, out, low), 0)

    return pl.pallas_call(
        body,
        out_shape=(jax.ShapeDtypeStruct((rows // 2, HD), BF),) * 2,
        scratch_shapes=[pltpu.VMEM((2 * HD, WINDOW + rows), BF)],
        compiler_params=BIG,
        name="attention",
    )(query, own, other, bias)


def small_expm1(y):
    near = y * (
        1.0
        + y * (1 / 2)
        * (1.0 + y * (1 / 3) * (1.0 + y * (1 / 4) * (1.0 + y * (1 / 5) * (1.0 + y * (1 / 6)
        * (1.0 + y * (1 / 7) * (1.0 + y * (1 / 8) * (1.0 + y * (1 / 9) * (1.0 + y * (1 / 10)))))))))
    )
    return jnp.where(y > -1.0, near, jnp.exp(y) - 1.0)


def scan_body(to_branch, inner, squares, halo, taps, w_rate, w_admit, rate_scale, lsb, cub, ends, ext, prior, dec, sca, lanes_in):
    rows = inner.shape[0]
    wide = lanes_in
    ext[0:8, :] = halo[...]
    seg = rows // 8
    parts = range(wide // 128)

    def scaled_in(i, _):
        here = pl.ds(pl.multiple_of(i * 128, 128), 128)
        r = lax.rsqrt(squares[here, :] * (1.0 / 4096.0) + EPSILON)
        ext[pl.ds(pl.multiple_of(i * 128 + 8, 8), 128), :] = inner[here, :] * r
        return 0

    lax.fori_loop(0, rows // 128, scaled_in, 0)

    def gates(i, _):
        here = pl.ds(pl.multiple_of(i * 128, 128), 128)
        around_here = ext[pl.ds(pl.multiple_of(i * 128, 128), 136), :]
        conv = taps[0:1, :] * around_here[8:136]
        for tap in range(1, 4):
            conv = conv + taps[tap : tap + 1, :] * around_here[8 - tap : 136 - tap]
        low = conv.astype(BF)
        rate = jax.nn.sigmoid(dot32(low, w_rate[...]))
        log_decay = rate * rate_scale[...]
        decay = jnp.exp(log_decay)
        admit = jax.nn.sigmoid(dot32(low, w_admit[...]))
        scaled = admit * conv * jnp.sqrt(-small_expm1(2.0 * log_decay))
        for n in parts:
            dec[n][here, :] = decay[:, n * 128 : (n + 1) * 128]
            sca[n][here, :] = scaled[:, n * 128 : (n + 1) * 128]
        return 0

    lax.fori_loop(0, rows // 128, gates, 0)
    c = [dec[n][pl.ds(0, 8, stride=seg), :] for n in parts]
    h = [sca[n][pl.ds(0, 8, stride=seg), :] for n in parts]
    for t in range(1, seg):
        for n in parts:
            d = dec[n][pl.ds(t, 8, stride=seg), :]
            h[n] = d * h[n] + sca[n][pl.ds(t, 8, stride=seg), :]
            c[n] = c[n] * d
            dec[n][pl.ds(t, 8, stride=seg), :] = c[n]
            sca[n][pl.ds(t, 8, stride=seg), :] = h[n]
    c, h = jnp.concatenate(c, axis=1), jnp.concatenate(h, axis=1)
    before_h = jnp.zeros((1, wide), F32)
    before_c = jnp.ones((1, wide), F32)
    befores = []
    for g in range(8):
        befores.append((before_h, before_c))
        before_h = h[g : g + 1, :] + c[g : g + 1, :] * before_h
        before_c = c[g : g + 1, :] * before_c
    prior[0:8, :] = jnp.concatenate([p[0] for p in befores], axis=0)
    prior[8:16, :] = jnp.concatenate([p[1] for p in befores], axis=0)

    def joined(g, _):
        here = pl.ds(pl.multiple_of(g * seg, seg), seg)
        r = lax.rsqrt(squares[here, :] * (1.0 / 4096.0) + EPSILON)
        branch = jax.nn.gelu(to_branch[here, :] * r)
        cum = jnp.concatenate([dec[n][here, :] for n in parts], axis=1)
        state = jnp.concatenate([sca[n][here, :] for n in parts], axis=1)
        lsb[here, :] = (state + cum * prior[pl.ds(g, 1), :]) * branch
        cub[here, :] = cum * prior[pl.ds(g + 8, 1), :] * branch
        return 0

    lax.fori_loop(0, 8, joined, 0)
    for k in range(ends.shape[0]):
        ends[k, 0:1, :] = before_c
        ends[k, 1:2, :] = before_h


def local_scan(to_branch, inner, squares, halo, taps, w_rate, w_admit, rate_scale, copies):
    rows, wide = inner.shape

    def body(*refs):
        scan_body(*refs, wide)

    return pl.pallas_call(
        body,
        out_shape=(
            jax.ShapeDtypeStruct((rows, wide), F32),
            jax.ShapeDtypeStruct((rows, wide), F32),
            jax.ShapeDtypeStruct((copies, 2, wide), F32),
        ),
        scratch_shapes=[
            pltpu.VMEM((rows + 8, wide), F32),
            pltpu.VMEM((16, wide), F32),
            [pltpu.VMEM((rows, 128), F32)] * (wide // 128),
            [pltpu.VMEM((rows, 128), F32)] * (wide // 128),
        ],
        compiler_params=pltpu.CompilerParams(vmem_limit_bytes=VMEM_BYTES),
        name="local_scan",
    )(to_branch, inner, squares, halo, taps, w_rate, w_admit, rate_scale)


def apply_carry(lsb, cub, pieces, mine):
    def body(at, lsb, cub, pieces, out):
        carry = jnp.zeros((1, lsb.shape[1]), F32)
        for k in range(pieces.shape[0]):
            fresh = pieces[k, 1:2, :] + pieces[k, 0:1, :] * carry
            carry = jnp.where(k < at[0], fresh, carry)
        out[...] = (lsb[...] + cub[...] * carry).astype(BF)

    vm = pl.BlockSpec(memory_space=pltpu.VMEM)
    return pl.pallas_call(
        body,
        in_specs=[pl.BlockSpec(memory_space=pltpu.SMEM), vm, vm, vm],
        out_specs=vm,
        out_shape=jax.ShapeDtypeStruct(lsb.shape, BF),
        compiler_params=pltpu.CompilerParams(vmem_limit_bytes=VMEM_BYTES),
        name="apply_carry",
    )(mine, lsb, cub, pieces)


def on_device(
    tokens, w_branch, w_input, conv_kernel, w_rate, w_admit, lam, w_out, w_query, w_key, w_value, w_attn_out
):
    batch, rows, cols = tokens.shape
    width = w_branch.shape[0]
    n_mp, n_ctx = lax.axis_size("mp"), lax.axis_size("ctx")
    z, j = lax.axis_index("mp"), lax.axis_index("ctx")
    z, j, core, base, first_seen, tokens = lax.optimization_barrier(
        (z, j, lax.rem(j, 2), j * rows, WINDOW - j * rows, tokens)
    )
    lru = w_branch.shape[1]
    x = tokens.reshape(rows, cols)

    zs, cores = z.reshape(1), core.reshape(1)
    half = n_mp // 2
    each = w_key.shape[1]
    part = w_out.shape[0] // n_ctx

    def lines_of(w):
        return lax.dynamic_slice_in_dim(w, j * part, part, 0)

    def along_ctx(a):
        return lax.all_gather(a, "ctx", axis=0)

    def in_order(a):
        whole = a.reshape(n_ctx, n_mp, part, a.shape[-1]).transpose(1, 0, 2, 3)
        return whole.reshape(n_mp * n_ctx * part, a.shape[-1])

    lines = jnp.stack([lines_of(w_out), lines_of(w_attn_out)]).reshape(2, part, n_mp, cols)
    lines = lines.transpose(0, 2, 1, 3).reshape(2 * n_mp * part, cols)

    tall = (rows + lines.shape[0]) // 2

    def joined_weights(found, made):
        return jnp.concatenate([w_query, w_key, w_value, jnp.zeros((width, 128 - 2 * each), BF)], axis=1)

    def tables(found, made):
        here, _ = lax.optimization_barrier((base, found[1][0]))
        span = WINDOW + rows
        freqs = 10000.0 ** (-jnp.arange(HD // 4, dtype=F32) * 2.0 / (HD // 2))
        slots = jnp.concatenate([jnp.arange(rows, dtype=jnp.int32) - back * rows for back in (0, 2, 4)])
        angles = freqs[:, None] * (here + slots).astype(F32)[None, :]
        cos_k, sin_k = jnp.cos(angles), jnp.sin(angles)
        bias = jnp.where(jnp.arange(span, dtype=jnp.int32) >= first_seen, 0.0, -1e30).astype(F32)[None]
        rate_scale = (-8.0 * jax.nn.softplus(-lam)).reshape(1, lru)
        return cos_k, sin_k, bias, rate_scale

    def first_part(found, made):
        return first_dots(zs, found, None, n_mp, w_branch, w_input, rows)

    of_x, made = ring_pieces([x[:tall], jnp.concatenate([x[tall:], lines], axis=0)], "mp", 0, {1: joined_weights, 2: tables, 3: first_part})
    w_qkv = made[1]
    cos_k, sin_k, bias, rate_scale = made[2]
    near_x = nearest(of_x, n_mp, half - 2)
    to_branch, inner, squares, tail = first_dots(zs, others(of_x, near_x), made[3], n_mp, w_branch, w_input, rows)

    with_lines = {k: (v[-1], rows - (0 if len(v) == 1 else v[0].shape[0])) for k, v in of_x.items()}
    zs_late, tail = lax.optimization_barrier((zs, tail))
    products, last_lines = line_products(zs_late, with_lines, n_mp, w_qkv, part)
    w_second = along_ctx(products)
    halo = from_behind(tail, "ctx", 1)

    lsb, cub, ends = local_scan(
        to_branch, inner, squares, halo, conv_kernel, w_rate[0], w_admit[0], rate_scale, n_ctx
    )
    last_lines, ends = lax.optimization_barrier((last_lines, ends))
    w_last = along_ctx(last_lines)
    carried = lax.all_to_all(ends, "ctx", split_axis=0, concat_axis=0, tiled=True)
    gated = apply_carry(lsb, cub, carried, j.reshape(1))

    def after(value, found):
        flat, tree = jax.tree.flatten(value)
        *flat, _ = lax.optimization_barrier((*flat, found[0][0]))
        return jax.tree.unflatten(tree, flat)

    def some_of_x(found, made):
        return one_dot("first_qkv", zs, after(near_x, found), None, n_mp, w_qkv, rows)

    def rest_of_x(found, made):
        return one_dot("first_qkv", zs, others(of_x, near_x), made[1], n_mp, w_qkv, rows)

    def second_weights(found, made):
        return in_order(after(w_second, {0: [found[1][0]]}))

    def some_second(found, made):
        return one_dot("second", zs, nearest(found, n_mp, half - 2), None, n_mp, made[3], rows)

    pieces, made = ring_pieces(
        gated, "mp", 0, {1: some_of_x, 2: rest_of_x, 3: second_weights, 4: some_second}
    )
    late = others(pieces, nearest(pieces, n_mp, half - 2))
    q_raw, block, resid = middle(zs, late, made[4], made[2], x, n_mp, made[3], each)

    def last_weights(found, made):
        return in_order(after(w_last, {0: [found[2][0]]}))

    four = from_behind(block, "ctx", 4)
    line = jnp.concatenate([block, from_behind(block, "ctx", 2), four], axis=1)
    near, made = ring_pieces(line, "mp", 1, {3: last_weights})
    w_last = made[3]
    own, sent, r = window(zs, cores, near, {k: [] for k in near}, cos_k, sin_k, n_mp, each)
    other = lax.ppermute(sent, "ctx", [(i, i ^ 1) for i in range(n_ctx)])
    query = make_query(q_raw, r, cos_k, sin_k)
    attended = attention(query, own, other, bias)

    def some_last(found, made):
        return one_dot("third", zs, nearest(found, n_mp, half - 2), None, n_mp, w_last, rows)

    pieces, made = ring_pieces(list(attended), "mp", 0, {3: some_last})
    late = others(pieces, nearest(pieces, n_mp, half - 2))
    last = last_dot(zs, late, made[3], resid, n_mp, w_last)
    return last.reshape(batch, rows, cols)


def solution(mesh):
    in_specs = (
        P(None, "ctx", "mp"),
        P(None, "mp"),
        P(None, "mp"),
        P(None, "mp"),
        P("mp", None, None),
        P("mp", None, None),
        P("mp"),
        P("mp", None),
        P(None, "mp"),
        P(None, "mp"),
        P(None, "mp"),
        P("mp", None),
    )
    return jax.shard_map(
        on_device, mesh=mesh, in_specs=in_specs, out_specs=P(None, "ctx", "mp"), check_vma=False
    )
```
